32 devices in a mesh: rows: 16 (over z, x, core), seq: 2 (over y).
Axes of the slice: x: 2, y: 2, z: 4, core: 2. Of those that a mesh axis runs over, the one named last changes fastest.
Arguments:
- tokens: bfloat16 [16, 1888, 768], P('rows', 'seq'), may hold values from -6 to 6
- cotangent: bfloat16 [16, 1888, 768], P('rows', 'seq'), may hold values from -6 to 6
- segment_ids: int32 [16, 1888], P('rows'), may hold values from 0 to 3, as said below
- routing: int32 [16, 1888], P('rows'), may hold values from 0 to 943, as said below
- qkv_weight: bfloat16 [768, 2304], replicated, may hold values from -0.21875 to 0.21875
- query_bias: bfloat16 [768], replicated, may hold values from -1 to 1
- value_bias: bfloat16 [768], replicated, may hold values from -1 to 1
- out_weight: bfloat16 [768, 768], replicated, may hold values from -0.875 to 0.875
- out_bias: bfloat16 [768], replicated, may hold values from -1 to 1
- first_scale: bfloat16 [768], replicated, may hold values from 0.5 to 1.5
- first_offset: bfloat16 [768], replicated, may hold values from -1 to 1
- second_scale: bfloat16 [768], replicated, may hold values from 0.5 to 1.5
- second_offset: bfloat16 [768], replicated, may hold values from -1 to 1
- up_weight: bfloat16 [768, 3072], replicated, may hold values from -0.21875 to 0.21875
- up_bias: bfloat16 [3072], replicated, may hold values from -1 to 1
- down_weight: bfloat16 [3072, 768], replicated, may hold values from -0.109375 to 0.109375
- down_bias: bfloat16 [768], replicated, may hold values from -1 to 1
- router_weight: bfloat16 [768], replicated, may hold values from -0.21875 to 0.21875
Outputs:
- out_tokens: bfloat16 [16, 1888, 768], P('rows', 'seq')
- grad_tokens: bfloat16 [16, 1888, 768], P('rows', 'seq')
- grad_qkv_weight: float32 [768, 2304], replicated
- grad_query_bias: float32 [768], replicated
- grad_value_bias: float32 [768], replicated
- grad_out_weight: float32 [768, 768], replicated
- grad_out_bias: float32 [768], replicated
- grad_first_scale: float32 [768], replicated
- grad_first_offset: float32 [768], replicated
- grad_second_scale: float32 [768], replicated
- grad_second_offset: float32 [768], replicated
- grad_up_weight: float32 [768, 3072], replicated
- grad_up_bias: float32 [3072], replicated
- grad_down_weight: float32 [3072, 768], replicated
- grad_down_bias: float32 [768], replicated
- grad_router_weight: float32 [768], replicated
The draws below stay inside these ranges and needn't reach their ends.
Inputs may be any that keep to these rules, and one draw needn't show every extreme that they name: `segment_ids`: in each row the ids start at 0 and rise by one at each new image; every image but a row's first and last has 577 slots, and the image that holds slot 944 also holds slot 943. `routing`: each aligned block of 944 entries of a row is an order of 0 to 943.
All inputs are finite; a program needn't handle non-finite values.
Results may differ from the reference program's by a relative error of at most 0.012.
Values may be sent and summed in bfloat16 or wider, within the bound.
No kernel may reach another device: no remote copies, remote signals or barrier semaphores. Data moves between devices by JAX's collectives and lax.ppermute only.
A program may use at most 192 MiB of HBM per device.

```python
import jax
import jax.numpy as jnp
from jax import lax

D = 768
H = 12
HD = 64
FF = 3072
IMG = 577
SLOT_DEV = 944
R_DEV = 472
ROWS = 16
SLOTS = 1888


def draw_segment_ids(key, part):
    start_gap = jax.random.randint(key, (ROWS, 1), IMG // 4, IMG - IMG // 4, dtype=jnp.int32)
    first_start = SLOT_DEV - start_gap
    phase_shift = (IMG - first_start % IMG) % IMG
    slot_index = jnp.arange(SLOTS, dtype=jnp.int32)[None, :]
    raw_ids = ((slot_index + phase_shift) // IMG).astype(jnp.int32)
    return jnp.minimum(raw_ids, (SLOTS - 1) // IMG).astype(jnp.int32)


def draw_routing(key, part):
    blocks = ROWS * (SLOTS // SLOT_DEV)
    block_keys = jax.random.split(key, blocks)
    orders = jax.vmap(lambda block_key: jax.random.permutation(block_key, SLOT_DEV))(block_keys)
    return orders.reshape(ROWS, SLOTS).astype(jnp.int32)


def steps_of(key, shape, cuts, low, high):
    def one(dim, blocks):
        draws = jax.random.uniform(jax.random.fold_in(jax.random.fold_in(key, 6), dim), (blocks,), jnp.float32, low / len(cuts), high / len(cuts))
        return jnp.repeat(jnp.exp(draws), shape[dim] // blocks).reshape((-1,) + (1,) * (len(shape) - dim - 1))

    gain = one(*cuts[0])
    for cut in cuts[1:]:
        gain = gain * one(*cut)
    return gain


def bell_draw(own_key, extent, deviation, most, pieces=(), kind=jnp.bfloat16):
    factor_of = steps_of(own_key, extent, pieces, -0.22, 0.18) if pieces else 1.0
    values = jax.random.normal(own_key, extent, jnp.float32) * deviation * factor_of
    return jnp.minimum(jnp.maximum(values, -most), most).astype(kind)


def setup_inputs(seed: int = 0) -> dict:
    key_of = jax.random.split(jax.random.key(seed), 19)
    tokens = bell_draw(key_of[0], (ROWS, SLOTS, D), 1.0, 6.0, ((0, 16), (1, 2)))
    cotangent = bell_draw(key_of[1], (ROWS, SLOTS, D), 1.0, 6.0, ((0, 16), (1, 2)))
    segment_ids = draw_segment_ids(jax.random.fold_in(key_of[18], 71), 0)
    routing = draw_routing(jax.random.fold_in(key_of[18], 71), 0)
    qkv_weight = bell_draw(key_of[4], (D, 3 * D), D ** -0.5, 0.21875)
    query_bias = bell_draw(key_of[5], (D,), 0.2, 1.0)
    value_bias = bell_draw(key_of[6], (D,), 0.2, 1.0)
    out_weight = bell_draw(key_of[7], (D, D), (D // 16) ** -0.5, 0.875)
    out_bias = bell_draw(key_of[8], (D,), 0.2, 1.0)
    first_scale = jnp.clip(1.0 + 0.1 * jax.random.normal(key_of[9], (D,), jnp.float32), 0.5, 1.5).astype(jnp.bfloat16)
    first_offset = bell_draw(key_of[10], (D,), 0.2, 1.0)
    second_scale = jnp.clip(1.0 + 0.1 * jax.random.normal(key_of[11], (D,), jnp.float32), 0.5, 1.5).astype(jnp.bfloat16)
    second_offset = bell_draw(key_of[12], (D,), 0.2, 1.0)
    up_weight = bell_draw(key_of[13], (D, FF), D ** -0.5, 0.21875)
    up_bias = bell_draw(key_of[14], (FF,), 0.2, 1.0)
    down_weight = bell_draw(key_of[15], (FF, D), FF ** -0.5, 0.109375)
    down_bias = bell_draw(key_of[16], (D,), 0.2, 1.0)
    router_weight = bell_draw(key_of[17], (D,), D ** -0.5, 0.21875)
    return {"tokens": tokens, "cotangent": cotangent, "segment_ids": segment_ids, "routing": routing, "qkv_weight": qkv_weight, "query_bias": query_bias, "value_bias": value_bias, "out_weight": out_weight, "out_bias": out_bias, "first_scale": first_scale, "first_offset": first_offset, "second_scale": second_scale, "second_offset": second_offset, "up_weight": up_weight, "up_bias": up_bias, "down_weight": down_weight, "down_bias": down_bias, "router_weight": router_weight}


@jax.custom_vjp
def low(v):
    return lax.optimization_barrier(v.astype(jnp.bfloat16)).astype(jnp.float32)

@jax.custom_vjp
def low_back(v):
    return v

def low_keep(v):
    return (low(v), None)

def low_pass(kept, grad):
    return (grad,)

def back_keep(v):
    return (v, None)

def back_low(kept, grad):
    return (low(grad),)
low.defvjp(low_keep, low_pass)
low_back.defvjp(back_keep, back_low)

def layer_norm(values, scaling, offset):
    center = values - lax.optimization_barrier(jnp.mean(values, axis=-1, keepdims=True))
    inverse = lax.rsqrt(lax.optimization_barrier(jnp.mean(center * center, axis=-1, keepdims=True)) + 1e-06)
    return center * inverse * scaling + offset

def gelu_tanh(activation):
    return jax.nn.gelu(activation, approximate=True)

def row_forward(weights, row_tokens, row_segments, row_routing):
    qkv_weight, query_bias, value_bias, out_weight, out_bias, first_scale, first_offset, second_scale, second_offset, up_weight, up_bias, down_weight, down_bias, router_weight = weights
    highest = lax.Precision.HIGHEST
    model_width = row_tokens.shape[1]
    halves = row_tokens.shape[0] // SLOT_DEV
    starts = jnp.arange(halves, dtype=jnp.int32)[:, None] * SLOT_DEV
    chosen = (row_routing.reshape(halves, SLOT_DEV)[:, :R_DEV] + starts).reshape(-1).astype(jnp.int32)
    routed_in = row_tokens[chosen]
    segments = row_segments[chosen]
    routed_count = routed_in.shape[0]
    gate_value = jax.nn.sigmoid(jnp.dot(routed_in, router_weight, precision=highest))
    first_norm = low(layer_norm(routed_in, first_scale, first_offset))
    projected = jnp.dot(first_norm, qkv_weight, precision=highest)
    queries = low(low_back(projected[:, :model_width] + query_bias))
    key_rows = low(low_back(projected[:, model_width:2 * model_width]))
    values = low(low_back(projected[:, 2 * model_width:] + value_bias))
    queries = queries.reshape(routed_count, H, HD)
    key_rows = key_rows.reshape(routed_count, H, HD)
    values = values.reshape(routed_count, H, HD)
    scores = low_back(jnp.einsum('qhd,khd->hqk', queries, key_rows, precision=highest) * HD ** (-0.5))
    allowed = segments[:, None] == segments[None, :]
    scores = jnp.where(allowed[None], scores, -jnp.inf)
    row_top = lax.optimization_barrier(jnp.max(scores, axis=-1, keepdims=True))
    exponent = jnp.exp(scores - row_top)
    attention_weights = exponent / lax.optimization_barrier(jnp.sum(exponent, axis=-1, keepdims=True))
    attended = jnp.einsum('hqk,khd->qhd', low(attention_weights), values, precision=highest)
    attended = low(low_back(attended.reshape(routed_count, model_width)))
    branch_attention = low_back(jnp.dot(attended, out_weight, precision=highest) + out_bias)
    mixed_sum = routed_in + branch_attention
    second_norm = low(layer_norm(mixed_sum, second_scale, second_offset))
    hidden_pre = low_back(jnp.dot(second_norm, up_weight, precision=highest) + up_bias)
    hidden_low = low(gelu_tanh(hidden_pre))
    branch_feed = low_back(jnp.dot(hidden_low, down_weight, precision=highest) + down_bias)
    routed_out = routed_in + gate_value[:, None] * (branch_attention + branch_feed)
    return row_tokens.at[chosen].set(routed_out)

def reference(tokens, cotangent, segment_ids, routing, qkv_weight, query_bias, value_bias, out_weight, out_bias, first_scale, first_offset, second_scale, second_offset, up_weight, up_bias, down_weight, down_bias, router_weight):
    weight_list = (qkv_weight, query_bias, value_bias, out_weight, out_bias, first_scale, first_offset, second_scale, second_offset, up_weight, up_bias, down_weight, down_bias, router_weight)
    floats = tuple((member.astype(jnp.float32) for member in weight_list))
    row_step = jax.checkpoint(row_forward)

    def forward(token_float, *weights):

        def scan_body(unused_carry, inputs):
            return (unused_carry, row_step(weights, inputs[0], inputs[1], inputs[2]))
        _, result = lax.scan(scan_body, jnp.zeros((), jnp.float32), (token_float, segment_ids, routing))
        return result
    result, backward = jax.vjp(forward, tokens.astype(jnp.float32), *floats)
    gradients = backward(cotangent.astype(jnp.float32))
    return (result.astype(jnp.bfloat16), gradients[0].astype(jnp.bfloat16), gradients[1], gradients[2], gradients[3], gradients[4], gradients[5], gradients[6], gradients[7], gradients[8], gradients[9], gradients[10], gradients[11], gradients[12], gradients[13], gradients[14])
```

```python
import jax
import jax.numpy as jnp
from jax import lax
from jax.sharding import PartitionSpec as P

H = 12
HD = 64


def from_behind(block, axis, distance):
    devices = range(lax.axis_size(axis))
    route = [((i - distance) % len(devices), i) for i in devices]
    return lax.ppermute(block, axis, route)


def layer_norm(values, scaling, offset):
    center = values - jnp.mean(values, axis=-1, keepdims=True)
    inverse = lax.rsqrt(jnp.mean(center * center, axis=-1, keepdims=True) + 1e-06)
    return center * inverse * scaling + offset


def gelu_tanh(activation):
    return jax.nn.gelu(activation, approximate=True)


def pick_rows(source_rows, indices):
    return jnp.take_along_axis(source_rows, indices[:, :, None], axis=1)


def masked_scores(queries, key_rows, query_segment, key_segment):
    scores = jnp.einsum(
        "rqhd,rkhd->rhqk", queries, key_rows, preferred_element_type=jnp.float32
    ) * HD ** (-0.5)
    allowed = (query_segment[:, :, None] == key_segment[:, None, :])[:, None]
    return jnp.where(allowed, scores, -jnp.inf)


def bit_partner(row, seq, axis):
    if axis == "y":
        return row, seq ^ 1
    return row ^ {"c": 1, "x": 2, "z1": 4, "z2": 8}[axis], seq


def swap(block, axes):
    rows = lax.axis_size("rows")
    route = []
    for row in range(rows):
        for seq in range(2):
            other_row, other_seq = bit_partner(row, seq, axes[row & 1])
            route.append((row * 2 + seq, other_row * 2 + other_seq))
    return lax.ppermute(block, ("rows", "seq"), route)


def own_bit(axis):
    if axis == "y":
        return lax.axis_index("seq")
    shift = {"c": 0, "x": 1, "z1": 2, "z2": 3}[axis]
    return (lax.axis_index("rows") >> shift) & 1


def stage_bit(axes):
    if axes[0] == axes[1]:
        return own_bit(axes[0])
    return jnp.where(own_bit("c") == 0, own_bit(axes[0]), own_bit(axes[1]))


def half_of(block, which):
    half = block.shape[0] // 2
    return lax.dynamic_slice_in_dim(block, which * half, half, 0)


def add_low(left, right):
    return (left.astype(jnp.float32) + right.astype(jnp.float32)).astype(jnp.bfloat16)


def reduce_rows(left_half, right_half, stages):
    core = own_bit("c")
    send = jnp.where(core == 0, right_half, left_half)
    keep = jnp.where(core == 0, left_half, right_half)
    got = swap(send, ("c", "c"))
    for axes in stages:
        bit = stage_bit(axes)
        send = add_low(half_of(keep, 1 - bit), half_of(got, 1 - bit))
        keep_next = add_low(half_of(keep, bit), half_of(got, bit))
        got = swap(send, axes)
        keep = keep_next
    total = add_low(keep, got)
    extra = 16
    while extra < lax.axis_size("rows"):
        size = lax.axis_size("rows")
        route = [(i * 2 + j, (i ^ extra) * 2 + j) for i in range(size) for j in range(2)]
        total = add_low(total, lax.ppermute(total, ("rows", "seq"), route))
        extra *= 2
    return total


def gather_rows(block, stages):
    for axes in reversed(stages):
        bit = stage_bit(axes)
        got = swap(block, axes)
        block = jnp.where(
            bit == 0, jnp.concatenate([block, got]), jnp.concatenate([got, block])
        )
    return block


def join_cores(block):
    got = swap(block, ("c", "c"))
    core = own_bit("c")
    return jnp.where(core == 0, block, got), jnp.where(core == 0, got, block)


XY_FIRST = (("x", "y"), ("y", "x"), ("z1", "z1"), ("z2", "z2"))
Z_FIRST = (("z1", "z1"), ("x", "y"), ("y", "x"), ("z2", "z2"))


def body(
    tokens,
    cotangent,
    segment_ids,
    routing,
    qkv_weight,
    query_bias,
    value_bias,
    out_weight,
    out_bias,
    first_scale,
    first_offset,
    second_scale,
    second_offset,
    up_weight,
    up_bias,
    down_weight,
    down_bias,
    router_weight,
):
    row_count, slot_count, model_width = tokens.shape
    hidden_width = up_weight.shape[1]
    routed_count = slot_count // 2
    head_shape = (row_count, routed_count, H, HD)
    flat_shape = (row_count, routed_count, model_width)
    position = lax.axis_index("seq")
    other_position = 1 - position
    own_route = lax.dynamic_slice_in_dim(routing, position * slot_count, slot_count, 1)
    other_route = lax.dynamic_slice_in_dim(routing, other_position * slot_count, slot_count, 1)
    own_groups = lax.dynamic_slice_in_dim(segment_ids, position * slot_count, slot_count, 1)
    other_groups = lax.dynamic_slice_in_dim(segment_ids, other_position * slot_count, slot_count, 1)
    chosen = own_route[:, :routed_count]
    query_segment = jnp.take_along_axis(own_groups, chosen, axis=1)
    remote_segment = jnp.take_along_axis(other_groups, other_route[:, :routed_count], axis=1)
    norm_one = (first_scale.astype(jnp.float32), first_offset.astype(jnp.float32))
    norm_two = (second_scale.astype(jnp.float32), second_offset.astype(jnp.float32))
    routed_in = pick_rows(tokens, chosen)
    routed_float = routed_in.astype(jnp.float32)
    router_logit = jnp.einsum(
        "rtd,d->rt", routed_in, router_weight, preferred_element_type=jnp.float32
    )
    gate_value = jax.nn.sigmoid(router_logit)
    first_norm = layer_norm(routed_float, norm_one[0], norm_one[1]).astype(jnp.bfloat16)
    projected = jnp.einsum(
        "rtd,de->rte", first_norm, qkv_weight, preferred_element_type=jnp.float32
    )
    queries = (projected[..., :model_width] + query_bias).astype(jnp.bfloat16).reshape(head_shape)
    key_rows = (
        projected[..., model_width : 2 * model_width].astype(jnp.bfloat16).reshape(head_shape)
    )
    values = (
        (projected[..., 2 * model_width :] + value_bias).astype(jnp.bfloat16).reshape(head_shape)
    )
    received = from_behind(jnp.stack([key_rows, values]), "seq", 1)
    remote_keys = received[0]
    remote_values = received[1]
    local_scores = masked_scores(queries, key_rows, query_segment, query_segment)
    remote_scores = masked_scores(queries, remote_keys, query_segment, remote_segment)
    row_top = jnp.maximum(
        jnp.max(local_scores, axis=-1, keepdims=True),
        jnp.max(remote_scores, axis=-1, keepdims=True),
    )
    row_total = jnp.sum(jnp.exp(local_scores - row_top), axis=-1, keepdims=True) + jnp.sum(
        jnp.exp(remote_scores - row_top), axis=-1, keepdims=True
    )
    log_total = row_top + jnp.log(row_total)
    local_low = jnp.exp(local_scores - log_total).astype(jnp.bfloat16)
    remote_low = jnp.exp(remote_scores - log_total).astype(jnp.bfloat16)
    attended = jnp.einsum("rhqk,rkhd->rqhd", local_low, values, preferred_element_type=jnp.float32)
    attended = attended + jnp.einsum(
        "rhqk,rkhd->rqhd", remote_low, remote_values, preferred_element_type=jnp.float32
    )
    attended_low = attended.reshape(flat_shape).astype(jnp.bfloat16)
    branch_attention = (
        jnp.einsum("rtd,de->rte", attended_low, out_weight, preferred_element_type=jnp.float32)
        + out_bias
    )
    mixed_sum = routed_float + branch_attention
    second_norm = layer_norm(mixed_sum, norm_two[0], norm_two[1]).astype(jnp.bfloat16)
    hidden_pre = (
        jnp.einsum("rtd,df->rtf", second_norm, up_weight, preferred_element_type=jnp.float32)
        + up_bias
    )
    hidden_act, gelu_back = jax.vjp(gelu_tanh, hidden_pre)
    hidden_low = hidden_act.astype(jnp.bfloat16)
    branch_feed = (
        jnp.einsum("rtf,fd->rtd", hidden_low, down_weight, preferred_element_type=jnp.float32)
        + down_bias
    )
    branch_total = branch_attention + branch_feed
    routed_out = routed_float + gate_value[..., None] * branch_total
    row_ids = jnp.arange(row_count, dtype=jnp.int32)[:, None]
    out_tokens = tokens.at[row_ids, chosen].set(routed_out.astype(jnp.bfloat16))
    grad_routed = pick_rows(cotangent, chosen).astype(jnp.float32)
    logit_grad = jnp.sum(grad_routed * branch_total, axis=-1) * gate_value * (1.0 - gate_value)
    grad_router = jnp.einsum("rtd,rt->d", routed_float, logit_grad, precision=lax.Precision.HIGHEST)
    grad_delta = gate_value[..., None] * grad_routed
    grad_feed_low = grad_delta.astype(jnp.bfloat16)
    grad_down = jnp.einsum(
        "rtf,rtd->fd", hidden_low, grad_feed_low, preferred_element_type=jnp.float32
    )
    grad_down_vec = jnp.sum(grad_feed_low.astype(jnp.float32), axis=(0, 1))
    grad_hidden = jnp.einsum(
        "rtd,fd->rtf", grad_feed_low, down_weight, preferred_element_type=jnp.float32
    )
    grad_pre_low = gelu_back(grad_hidden)[0].astype(jnp.bfloat16)
    grad_up = jnp.einsum(
        "rtd,rtf->df", second_norm, grad_pre_low, preferred_element_type=jnp.float32
    )
    grad_up_vec = jnp.sum(grad_pre_low.astype(jnp.float32), axis=(0, 1))
    grad_second = jnp.einsum(
        "rtf,df->rtd", grad_pre_low, up_weight, preferred_element_type=jnp.float32
    )
    _, second_back = jax.vjp(layer_norm, mixed_sum, norm_two[0], norm_two[1])
    grad_mixed, grad_second_gain, grad_second_shift = second_back(grad_second)
    grad_attention_low = (grad_delta + grad_mixed).astype(jnp.bfloat16)
    grad_out = jnp.einsum(
        "rtd,rte->de", attended_low, grad_attention_low, preferred_element_type=jnp.float32
    )
    grad_out_vec = jnp.sum(grad_attention_low.astype(jnp.float32), axis=(0, 1))
    grad_attended = jnp.einsum(
        "rte,de->rtd", grad_attention_low, out_weight, preferred_element_type=jnp.float32
    )
    grad_attended = grad_attended.astype(jnp.bfloat16).reshape(head_shape)
    again = from_behind(jnp.stack([key_rows, values]), "seq", 1)
    back_keys = again[0]
    back_values = again[1]

    def block_grads(block_keys, block_values, key_segment):
        scores = masked_scores(queries, block_keys, query_segment, key_segment)
        block_weights = jnp.exp(scores - log_total)
        block_grad = jnp.einsum(
            "rqhd,rkhd->rhqk", grad_attended, block_values, preferred_element_type=jnp.float32
        )
        return (block_weights, block_grad)

    local_weights, local_grad = block_grads(key_rows, values, query_segment)
    remote_weights, remote_grad = block_grads(back_keys, back_values, remote_segment)
    row_dot = jnp.sum(local_weights * local_grad, axis=-1, keepdims=True) + jnp.sum(
        remote_weights * remote_grad, axis=-1, keepdims=True
    )
    local_dscore = (local_weights * (local_grad - row_dot)).astype(jnp.bfloat16)
    remote_dscore = (remote_weights * (remote_grad - row_dot)).astype(jnp.bfloat16)
    local_wlow = local_weights.astype(jnp.bfloat16)
    remote_wlow = remote_weights.astype(jnp.bfloat16)
    score_scale = HD ** (-0.5)
    grad_queries = score_scale * (
        jnp.einsum("rhqk,rkhd->rqhd", local_dscore, key_rows, preferred_element_type=jnp.float32)
        + jnp.einsum(
            "rhqk,rkhd->rqhd", remote_dscore, back_keys, preferred_element_type=jnp.float32
        )
    )
    remote_key_grad = score_scale * jnp.einsum(
        "rhqk,rqhd->rkhd", remote_dscore, queries, preferred_element_type=jnp.float32
    )
    remote_value_grad = jnp.einsum(
        "rhqk,rqhd->rkhd", remote_wlow, grad_attended, preferred_element_type=jnp.float32
    )
    returned = from_behind(jnp.stack([remote_key_grad, remote_value_grad]), "seq", -1)
    local_key_grad = score_scale * jnp.einsum(
        "rhqk,rqhd->rkhd", local_dscore, queries, preferred_element_type=jnp.float32
    )
    local_value_grad = jnp.einsum(
        "rhqk,rqhd->rkhd", local_wlow, grad_attended, preferred_element_type=jnp.float32
    )
    grad_query_low = grad_queries.reshape(flat_shape).astype(jnp.bfloat16)
    grad_key_low = (local_key_grad + returned[0]).reshape(flat_shape).astype(jnp.bfloat16)
    grad_value_low = (local_value_grad + returned[1]).reshape(flat_shape).astype(jnp.bfloat16)
    grad_projected = jnp.concatenate([grad_query_low, grad_key_low, grad_value_low], axis=-1)
    grad_qkv = jnp.einsum(
        "rtd,rte->de", first_norm, grad_projected, preferred_element_type=jnp.float32
    )
    grad_query_vec = jnp.sum(grad_query_low.astype(jnp.float32), axis=(0, 1))
    grad_value_vec = jnp.sum(grad_value_low.astype(jnp.float32), axis=(0, 1))
    grad_first = jnp.einsum(
        "rte,de->rtd", grad_projected, qkv_weight, preferred_element_type=jnp.float32
    )
    _, first_back = jax.vjp(layer_norm, routed_float, norm_one[0], norm_one[1])
    grad_from_norm, grad_first_gain, grad_first_shift = first_back(grad_first)
    grad_routed_in = (
        grad_routed
        + grad_mixed
        + grad_from_norm
        + logit_grad[..., None] * router_weight.astype(jnp.float32)
    )
    grad_tokens = cotangent.at[row_ids, chosen].set(grad_routed_in.astype(jnp.bfloat16))
    small = jnp.concatenate(
        [
            grad_query_vec,
            grad_value_vec,
            grad_out_vec,
            grad_first_gain,
            grad_first_shift,
            grad_router,
            grad_up_vec,
            grad_down_vec,
            grad_second_gain,
            grad_second_shift,
        ]
    )
    small_rows = small.shape[0] // 256
    small = small.reshape(2, small_rows, 128).astype(jnp.bfloat16)
    small = jnp.pad(small, ((0, 0), (0, model_width - small_rows), (0, 0)))
    half_width = model_width // 2
    half_hidden = hidden_width // 2
    half_qkv = 3 * half_width
    down_low = grad_down.astype(jnp.bfloat16)
    up_low = grad_up.astype(jnp.bfloat16)
    out_low = grad_out.astype(jnp.bfloat16)
    qkv_low = grad_qkv.astype(jnp.bfloat16)
    down_sum = reduce_rows(down_low[:, :half_width], down_low[:, half_width:], Z_FIRST)
    up_sum = reduce_rows(
        jnp.concatenate([up_low[:, :half_hidden], out_low[:, :half_width]], axis=1),
        jnp.concatenate([up_low[:, half_hidden:], out_low[:, half_width:]], axis=1),
        XY_FIRST,
    )
    qkv_sum = reduce_rows(
        jnp.concatenate([qkv_low[:, :half_qkv], small[0]], axis=1),
        jnp.concatenate([qkv_low[:, half_qkv:], small[1]], axis=1),
        XY_FIRST,
    )
    down_left, down_right = join_cores(gather_rows(down_sum, Z_FIRST))
    up_left, up_right = join_cores(gather_rows(up_sum, XY_FIRST))
    qkv_left, qkv_right = join_cores(gather_rows(qkv_sum, XY_FIRST))

    def wide(left, right):
        return jnp.concatenate([left, right], axis=1).astype(jnp.float32)

    small_sum = jnp.concatenate(
        [qkv_left[:small_rows, half_qkv:], qkv_right[:small_rows, half_qkv:]]
    )
    small_sum = small_sum.reshape(-1).astype(jnp.float32)
    pieces = [small_sum[i * model_width : (i + 1) * model_width] for i in range(6)]
    feed_small = small_sum[6 * model_width :]
    return (
        out_tokens,
        grad_tokens,
        wide(qkv_left[:, :half_qkv], qkv_right[:, :half_qkv]),
        pieces[0],
        pieces[1],
        wide(up_left[:, half_hidden:], up_right[:, half_hidden:]),
        pieces[2],
        pieces[3],
        pieces[4],
        feed_small[hidden_width + model_width : hidden_width + 2 * model_width],
        feed_small[hidden_width + 2 * model_width : hidden_width + 3 * model_width],
        wide(up_left[:, :half_hidden], up_right[:, :half_hidden]),
        feed_small[0:hidden_width],
        wide(down_left, down_right),
        feed_small[hidden_width : hidden_width + model_width],
        pieces[5],
    )


def solution(mesh):
    return jax.shard_map(
        body,
        mesh=mesh,
        in_specs=(
            P("rows", "seq", None),
            P("rows", "seq", None),
            P("rows", None),
            P("rows", None),
            P(),
            P(),
            P(),
            P(),
            P(),
            P(),
            P(),
            P(),
            P(),
            P(),
            P(),
            P(),
            P(),
            P(),
        ),
        out_specs=(
            P("rows", "seq", None),
            P("rows", "seq", None),
            P(),
            P(),
            P(),
            P(),
            P(),
            P(),
            P(),
            P(),
            P(),
            P(),
            P(),
            P(),
            P(),
            P(),
        ),
        check_vma=False,
    )
```

```python
import functools

import jax
import jax.numpy as jnp
from jax import lax
from jax.experimental import pallas as pl
from jax.experimental.pallas import tpu as pltpu
from jax.sharding import PartitionSpec as P

H = 12
HD = 64
PAIR = 2 * HD
TILE = 128
NEG = -1e30
SCALE = HD ** (-0.5)
UNIT = 100000
WEIGHT = {
    "pick_rows": 6 * UNIT,
    "near_attention": 16 * UNIT,
    "far_attention": 16 * UNIT,
    "feed_blocks": 13 * UNIT,
    "feed_grads": 7 * UNIT,
    "middle": 8 * UNIT,
    "own_back": 9 * UNIT,
    "other_back": 9 * UNIT,
    "last_grads": 8 * UNIT,
    "token_out": 7 * UNIT,
    "token_grad": 9 * UNIT,
}
F32 = jnp.float32
BF16 = jnp.bfloat16
I32 = jnp.int32
VMEM = pltpu.VMEM
SMEM = pltpu.SMEM


def nn(a, b):
    return lax.dot_general(a, b, (((1,), (0,)), ((), ())), preferred_element_type=F32)


def nt(a, b):
    return lax.dot_general(a, b, (((1,), (1,)), ((), ())), preferred_element_type=F32)


def tn(a, b):
    return lax.dot_general(a, b, (((0,), (0,)), ((), ())), preferred_element_type=F32)


def shape_of(shape, kind):
    return jax.ShapeDtypeStruct(shape, kind)


class Fetch:
    def __init__(self, source, target, sem):
        self.copy = pltpu.make_async_copy(source, target, sem)
        self.target, self.ready = target, False
        self.copy.start()

    def __call__(self):
        if not self.ready:
            self.copy.wait()
            self.ready = True
        return self.target


class Send:
    def __init__(self, buffer, target, sem):
        self.ref, self.target, self.sem = buffer, target, sem
        self.copy = pltpu.make_async_copy(buffer, target, sem)
        self.begun = False

    def go(self):
        self.copy.start()
        self.begun = True


def streamed(name, kernel, scalars, small, large, outs, scratch=(), scalar_outs=(), room=62):
    parts = []
    arrays = []
    for array, part, extent in large:
        at = next((i for i, a in enumerate(arrays) if a is array), None)
        if at is None:
            at = len(arrays)
            arrays.append(array)
        parts.append((at, part, extent))

    def wrapped(*refs):
        refs = list(refs)

        def take(count):
            head = refs[:count]
            del refs[:count]
            return head

        scalar_refs = take(len(scalars))
        small_refs = take(len(small))
        array_refs = take(len(arrays))
        out_refs = take(len(outs))
        scalar_out_refs = take(len(scalar_outs))
        landing = take(len(parts))
        staging = take(len(outs))
        in_sems, out_sems = take(2)
        fetches = []
        for i, (at, part, _) in enumerate(parts):
            source = array_refs[at] if part is None else part(array_refs[at], scalar_refs)
            fetches.append(Fetch(source, landing[i], in_sems.at[i]))
        sends = [Send(staging[i], out_refs[i], out_sems.at[i]) for i in range(len(outs))]
        kernel(scalar_refs, small_refs, fetches, sends, refs, scalar_out_refs)
        for fetch in fetches:
            fetch()
        for send in sends:
            if not send.begun:
                send.go()
        for send in sends:
            send.copy.wait()

    hbm = pl.BlockSpec(memory_space=pltpu.HBM)
    result = pl.pallas_call(
        wrapped,
        out_shape=tuple(outs) + tuple(scalar_outs),
        in_specs=[pl.BlockSpec(memory_space=SMEM)] * len(scalars)
        + [pl.BlockSpec(memory_space=VMEM)] * len(small)
        + [hbm] * len(arrays),
        out_specs=tuple([hbm] * len(outs) + [pl.BlockSpec(memory_space=SMEM)] * len(scalar_outs)),
        scratch_shapes=[VMEM(extent, arrays[at].dtype) for at, _, extent in parts]
        + [VMEM(o.shape, o.dtype) for o in outs]
        + [pltpu.SemaphoreType.DMA((len(parts),)), pltpu.SemaphoreType.DMA((len(outs),))]
        + list(scratch),
        compiler_params=pltpu.CompilerParams(vmem_limit_bytes=room << 20),
        cost_estimate=pl.CostEstimate(flops=0, bytes_accessed=WEIGHT[name], transcendentals=0),
        name=name,
    )(*scalars, *small, *arrays)
    return result


def full(array):
    return (array, None, array.shape)


def row_of(array, index):
    return (array, lambda ref, scalars: ref.at[index], array.shape[1:])


def head_rows(array, count):
    return (array, lambda ref, scalars: ref.at[0:count], (count,) + array.shape[1:])


def columns(array, start, count):
    return (array, lambda ref, scalars: ref.at[:, start : start + count], (array.shape[0], count))


def wide(ref):
    return ref[...].astype(F32)


def normalize(values):
    center = values - jnp.mean(values, axis=-1, keepdims=True)
    inverse = lax.rsqrt(jnp.mean(center * center, axis=-1, keepdims=True) + 1e-06)
    return center * inverse, inverse


def norm_back(grad, scale, unit, inverse):
    scaled = grad * scale
    first = jnp.mean(scaled, axis=-1, keepdims=True)
    second = jnp.mean(scaled * unit, axis=-1, keepdims=True)
    return inverse * (scaled - first - unit * second)


def tile_spans(line, count, out_ref):
    width = line.shape[1]
    lane = lax.broadcasted_iota(I32, (1, width), 1)
    tiles = width // TILE
    for i in range(tiles):
        inside = (lane >= i * TILE) & (lane < min((i + 1) * TILE, count))
        out_ref[i] = jnp.min(jnp.where(inside, line, 1e9)).astype(I32)
        out_ref[tiles + i] = jnp.max(jnp.where(inside, line, -1e9)).astype(I32)


def pick_rows(pos, routes, segs, tokens, cotangent, count, width):
    slots, depth = tokens.shape

    def kernel(scalars, small, fetches, sends, scratch, scalar_outs):
        route, seg, tok, cot = fetches
        routed, grad, hot_out = sends
        lane = lax.broadcasted_iota(I32, (slots, width), 1)
        slot = lax.broadcasted_iota(I32, (slots, width), 0)
        chosen = (slot == route()[:, :width]) & (lane < count)
        taken = jnp.max(jnp.where(chosen, 1.0, 0.0), axis=-1, keepdims=True)
        before = lax.broadcasted_iota(I32, (slots, slots), 0) < lax.broadcasted_iota(I32, (slots, slots), 1)
        before = jnp.where(before, 1.0, 0.0).astype(BF16)
        rank = tn(before, jnp.broadcast_to(taken, (slots, TILE)).astype(BF16))[:, 0:1]
        rank = jnp.where(taken > 0.0, rank, -1.0)
        hot = jnp.where(lane.astype(F32) == rank, 1.0, 0.0).astype(BF16)
        hot_out.ref[...] = hot
        hot_out.go()
        groups = jnp.broadcast_to(seg()[...].astype(F32), (8, slots)).astype(BF16)
        line = nn(groups, hot)
        line = jnp.where(lax.broadcasted_iota(I32, (8, width), 1) < count, line, -1.0)
        routed.ref[0:width] = tn(hot, tok()[...]).astype(BF16)
        routed.ref[width:] = jnp.zeros_like(routed.ref[width:])
        routed.ref[width : width + 8, 0:width] = line.astype(BF16)
        routed.go()
        grad.ref[...] = tn(hot, cot()[...]).astype(BF16)
        tile_spans(line[0:1], count, scalar_outs[0])

    return streamed(
        "pick_rows", kernel, [pos], [],
        [
            (routes, lambda ref, scalars: ref.at[scalars[0][0]], routes.shape[1:]),
            (segs, lambda ref, scalars: ref.at[scalars[0][0]], segs.shape[1:]),
            full(tokens), full(cotangent),
        ],
        [shape_of((width + 16, depth), BF16), shape_of((width, depth), BF16), shape_of((slots, width), BF16)],
        scalar_outs=[shape_of((2 * (width // TILE),), I32)],
    )


def key_span(keys, queries, j, tiles):
    low, high = queries[j], queries[tiles + j]
    first, last = jnp.int32(tiles), jnp.int32(-1)
    for t in range(tiles):
        meets = (keys[tiles + t] >= low) & (keys[t] <= high)
        first = jnp.where(meets & (first == tiles), t, first)
        last = jnp.where(meets, t, last)
    return jnp.minimum(first, tiles - 1), jnp.maximum(last - first + 1, 0)


def store_spans(ref, keys, queries, tiles):
    for j in range(tiles):
        first, many = key_span(keys, queries, j, tiles)
        ref[j] = first
        ref[tiles + j] = many


def fill_bias(bias_ref, key_line, query_line, key_pad):
    keys = jnp.where(key_line < 0.0, key_pad, key_line).T[:, 0:1]
    bias_ref[...] = jnp.where(keys == query_line[0:1], 0.0, NEG)


def stacked_heads(block):
    lane = lax.broadcasted_iota(I32, (1, PAIR), 1)
    zero = jnp.zeros_like(block)
    return jnp.concatenate([jnp.where(lane < HD, block, zero), jnp.where(lane >= HD, block, zero)], axis=0)


def own_blocks(block):
    return jnp.concatenate([block[0:HD, 0:TILE], block[HD:PAIR, TILE : 2 * TILE]], axis=0)


def twice(block):
    return jnp.concatenate([block, block], axis=1)


def over_tiles(span, tiles, pairs, lowest, work, group=3):
    def tile_step(j, carry):
        for n in range(lowest, tiles + 1):

            def branch(n=n):
                def group_step(i, inner):
                    for p in range(group):
                        work(n, j, i * group + p)
                    return inner

                lax.fori_loop(0, pairs // group, group_step, 0)

            pl.when(span[tiles + j] == n)(branch)
        return carry

    lax.fori_loop(0, tiles, tile_step, 0)


def project(normed, weights, qb, vb, q_ref, k_ref, v_ref, turned_ref, sends=None):
    depth = normed.shape[1]
    step = 256
    for part, (ref, weight) in enumerate(zip((k_ref, q_ref, v_ref), (weights[1], weights[0], weights[2]))):
        weight_ref = weight()
        for at in range(0, depth, step):
            value = nn(normed, weight_ref[:, at : at + step])
            if part == 1:
                value = value + qb[:, at : at + step]
            elif part == 2:
                value = value + vb[:, at : at + step]
            value = value.astype(BF16)
            ref[:, at : at + step] = value
            if part == 2:
                turned_ref[at : at + step, :] = value.T
        if sends is not None:
            sends[part].go()


def near_attention(spans, routed, qkv_weight, query_bias, value_bias, scale, offset, router):
    depth = routed.shape[1]
    width = routed.shape[0] - 16
    tiles = width // TILE
    pairs = depth // PAIR

    def kernel(scalars, small, fetches, sends, scratch, scalar_outs):
        qb, vb, scale_ref, offset_ref, router_ref = small
        q, k, v, normed, gate, acc, stat = sends
        bias, turned, span = scratch
        x_ref = fetches[0]()
        x = x_ref[0:width].astype(F32)
        unit, _ = normalize(x)
        low = (unit * wide(scale_ref) + wide(offset_ref)).astype(BF16)
        normed.ref[...] = low
        normed.go()
        logit = jnp.sum(x * wide(router_ref), axis=-1, keepdims=True)
        gate.ref[...] = jnp.broadcast_to(1.0 / (1.0 + jnp.exp(-logit)), gate.ref.shape)
        gate.go()
        project(low, fetches[1:4], wide(qb), wide(vb), q.ref, k.ref, v.ref, turned, (k, q, v))
        line = x_ref[width : width + 8, 0:width].astype(F32)
        fill_bias(bias, line, line, -1.0)
        store_spans(span, scalars[0], scalars[0], tiles)

        def work(n, j, pair):
            at = pl.multiple_of(pair * PAIR, PAIR)
            rows = pl.ds(pl.multiple_of(j * TILE, TILE), TILE)
            some = pl.ds(pl.multiple_of(span[j] * TILE, TILE), n * TILE)
            index = pair * tiles + j
            query = stacked_heads(q.ref[rows, pl.ds(at, PAIR)]) * SCALE
            scores = nt(k.ref[some, pl.ds(at, PAIR)], query) + twice(bias[some, rows])
            top = jnp.max(scores, axis=0, keepdims=True)
            weights = jnp.exp(scores - top)
            stat.ref[0, pl.ds(index, 1)] = top
            stat.ref[1, pl.ds(index, 1)] = jnp.sum(weights, axis=0, keepdims=True)
            acc.ref[index] = own_blocks(nn(turned[pl.ds(at, PAIR), some], weights.astype(BF16)))

        over_tiles(span, tiles, pairs, 1, work)

    low = shape_of((width, depth), BF16)
    return streamed(
        "near_attention", kernel, [spans], [query_bias, value_bias, scale, offset, router],
        [full(routed)] + [columns(qkv_weight, i * depth, depth) for i in range(3)],
        [
            low, low, low, low,
            shape_of((width, TILE), F32),
            shape_of((pairs * tiles, PAIR, TILE), F32),
            shape_of((2, pairs * tiles, 2 * TILE), F32),
        ],
        scratch=[VMEM((width, width), F32), VMEM((depth, width), BF16), SMEM((2 * tiles,), I32)],
    )


def far_attention(far, spans, routed, qkv_weight, query_bias, value_bias, scale, offset, count,
                  queries, acc, stat, out_weight, out_bias, scale2, offset2, gate, grad_routed, normed):
    depth = routed.shape[1]
    width = routed.shape[0] - 16
    tiles = width // TILE
    pairs = depth // PAIR

    def kernel(scalars, small, fetches, sends, scratch, scalar_outs):
        qb, vb, scale_ref, offset_ref, ob, scale2_ref, offset2_ref = small
        far_in, x_in, weight_q, weight_k, weight_v, q_in, acc_in, stat_in, ow, gate_in, grad_in, normed_in = fetches
        fq, fk, fv, pack, lse, branch_out, turned_out, lines = sends
        bias, turned, span, attended = scratch
        far_ref = far_in()
        far_line = far_ref[width : width + 8, 0:width].astype(F32)
        tile_spans(far_line[0:1], count, scalar_outs[0])
        unit, _ = normalize(far_ref[0:width].astype(F32))
        low = (unit * wide(scale_ref) + wide(offset_ref)).astype(BF16)
        project(low, (weight_q, weight_k, weight_v), wide(qb), wide(vb), fq.ref, fk.ref, fv.ref, turned,
                (fk, fq, fv))
        x_ref = x_in()
        line = x_ref[width : width + 8, 0:width].astype(F32)
        fill_bias(bias, far_line, line, -2.0)
        lines.ref[0] = line
        lines.ref[1] = jnp.where(far_line < 0.0, -2.0, far_line)
        lines.go()
        store_spans(span, scalar_outs[0], scalars[0], tiles)
        q_ref, acc_ref, stat_ref = q_in(), acc_in(), stat_in()

        def work(n, j, pair):
            at = pl.multiple_of(pair * PAIR, PAIR)
            rows = pl.ds(pl.multiple_of(j * TILE, TILE), TILE)
            index = pair * tiles + j
            one = pl.ds(index, 1)
            near, top, total = acc_ref[index], stat_ref[0, one], stat_ref[1, one]
            if n > 0:
                query = stacked_heads(q_ref[rows, pl.ds(at, PAIR)]) * SCALE
                some = pl.ds(pl.multiple_of(span[j] * TILE, TILE), n * TILE)
                scores = nt(fk.ref[some, pl.ds(at, PAIR)], query) + twice(bias[some, rows])
                near_top = top
                top = jnp.maximum(jnp.max(scores, axis=0, keepdims=True), near_top)
                weights = jnp.exp(scores - top)
                shrink = jnp.exp(near_top - top)
                total = jnp.sum(weights, axis=0, keepdims=True) + shrink * total
                value = own_blocks(nn(turned[pl.ds(at, PAIR), some], weights.astype(BF16)))
                near = value + jnp.concatenate(
                    [near[0:HD] * shrink[:, 0:TILE], near[HD:PAIR] * shrink[:, TILE:]], axis=0
                )
            part = jnp.concatenate([near[0:HD] / total[:, 0:TILE], near[HD:PAIR] / total[:, TILE:]], axis=0)
            attended[rows, pl.ds(at, PAIR)] = part.T.astype(BF16)
            lse.ref[one] = top + jnp.log(total)

        over_tiles(span, tiles, pairs, 0, work)
        pack.ref[2] = attended[...]
        pack.ref[3] = normed_in()[...]
        pack.ref[1] = (gate_in()[:, 0:1] * wide(grad_in())).astype(BF16)
        branch = nn(attended[...], ow()[...]) + wide(ob)
        branch_out.ref[...] = branch
        branch_out.go()
        unit, _ = normalize(x_ref[0:width].astype(F32) + branch)
        second = (unit * wide(scale2_ref) + wide(offset2_ref)).astype(BF16)
        pack.ref[0] = second
        pack.go()
        turned_out.ref[...] = second.T

    low = shape_of((width, depth), BF16)
    return streamed(
        "far_attention", kernel, [spans], [query_bias, value_bias, scale, offset, out_bias, scale2, offset2],
        [full(far), full(routed)] + [columns(qkv_weight, i * depth, depth) for i in range(3)]
        + [full(a) for a in (queries, acc, stat, out_weight, gate, grad_routed, normed)],
        [
            low, low, low,
            shape_of((4, width, depth), BF16),
            shape_of((pairs * tiles, 2 * TILE), F32),
            shape_of((width, depth), F32),
            shape_of((depth, width), BF16),
            shape_of((2, 8, width), F32),
        ],
        scratch=[
            VMEM((width, width), F32), VMEM((depth, width), BF16), SMEM((2 * tiles,), I32),
            VMEM((width, depth), BF16),
        ],
        scalar_outs=[shape_of((2 * tiles,), I32)],
    )


def feed_blocks(core, pack, up_weight, up_bias, down_weight, carried, pair):
    width, depth = pack.shape[1:]
    first = carried is None
    step = 256
    tiles = depth // step

    def block_of(which, scalars):
        other = 1 - scalars[0][0]
        return 2 * pair + (other if which == 0 else 1 - other)

    def up_part(which, i):
        def part(ref, scalars):
            start = pl.multiple_of(block_of(which, scalars) * depth + i * step, step)
            return ref.at[:, pl.ds(start, step)]
        return (up_weight, part, (depth, step))

    def down_part(which):
        def part(ref, scalars):
            return ref.at[pl.ds(pl.multiple_of(block_of(which, scalars) * depth, step), depth)]
        return (down_weight, part, (depth, depth))

    def kernel(scalars, small, fetches, sends, scratch, scalar_outs):
        second = fetches[0]
        gfl = fetches[1]
        ups = (fetches[2 : 2 + tiles], fetches[3 + tiles : 3 + 2 * tiles])
        downs = (fetches[2 + tiles], fetches[3 + 2 * tiles])
        rest = fetches[4 + 2 * tiles :]
        send, own, back_out, feed_out, vec_out = sends
        if first:
            vec_out.ref[...] = jnp.zeros_like(vec_out.ref)
            vec_out.ref[4:5, :] = jnp.sum(wide(gfl()), axis=0, keepdims=True)
        else:
            vec_out.ref[...] = rest[2]()[...]
        for which, out in enumerate((send, own)):
            block = block_of(which, scalars)
            down_ref = None
            for i in range(tiles):
                cols = slice(i * step, (i + 1) * step)
                start = pl.multiple_of(block * depth + i * step, step)
                pre = nn(second()[...], ups[which][i]()[...])
                pre = pre + small[0][:, pl.ds(start, step)].astype(F32)
                squared = pre * pre
                inner = pre * (0.7978845608028654 + 0.035677408136300125 * squared)
                tanh = jnp.tanh(inner)
                half = 0.5 + 0.5 * tanh
                out.ref[0, :, cols] = (pre * half).astype(BF16)
                slope = half + pre * (0.5 * (1.0 - tanh * tanh)) * (
                    0.7978845608028654 + 0.10703222440890037 * squared
                )
                if down_ref is None:
                    down_ref = downs[which]()
                grad = (nt(gfl()[...], down_ref[cols, :]) * slope).astype(BF16)
                out.ref[1, :, cols] = grad
                vec_out.ref[pl.ds(block, 1), cols] = jnp.sum(grad.astype(F32), axis=0, keepdims=True)
            out.go()
        for at in range(0, depth, step):
            cols = slice(at, at + step)
            value = nn(send.ref[0], downs[0]()[:, cols]) + nn(own.ref[0], downs[1]()[:, cols])
            if not first:
                value = value + rest[1]()[:, cols]
            feed_out.ref[:, cols] = value
        feed_out.go()
        value = None
        for which, out in enumerate((send, own)):
            for i in range(tiles):
                part = nt(out.ref[1, :, i * step : (i + 1) * step], ups[which][i]()[...])
                if value is None:
                    value = part if first else part + rest[0]()[...]
                else:
                    value = value + part
        back_out.ref[...] = value

    acts = shape_of((2, width, depth), BF16)
    total = shape_of((width, depth), F32)
    return streamed(
        "feed_blocks", kernel, [core], [up_bias],
        [row_of(pack, 0), row_of(pack, 1)]
        + [up_part(0, i) for i in range(tiles)] + [down_part(0)]
        + [up_part(1, i) for i in range(tiles)] + [down_part(1)]
        + ([] if first else [full(c) for c in carried]),
        [acts, acts, total, total, shape_of((16, depth), F32)],
    )


def feed_grads(got, bit, turned, pack, far_pack, own):
    depth, width = turned.shape
    step = 256

    def kernel(scalars, small, fetches, sends, scratch, scalar_outs):
        turned_in, far_second, own_grad, got_grad, gfl, far_gfl, own_hidden, got_hidden = fetches
        send, keep = sends
        both = scratch[0]
        bit = scalars[0][0]
        for at in range(0, depth, step):
            cols = slice(at, at + step)
            value = nn(turned_in()[...], own_grad()[:, cols]) + tn(far_second()[...], got_grad()[:, cols])
            both[bit, :, cols] = value.astype(BF16)
        for at in range(0, depth, step):
            rows = slice(at, at + step)
            value = tn(own_hidden()[:, rows], gfl()[...]) + tn(got_hidden()[:, rows], far_gfl()[...])
            both[1 - bit, rows, :] = value.astype(BF16)
        keep.copy = pltpu.make_async_copy(both.at[0], keep.target, keep.sem)
        send.copy = pltpu.make_async_copy(both.at[1], send.target, send.sem)
        keep.go()
        send.go()

    half = shape_of((depth, depth), BF16)
    return streamed(
        "feed_grads", kernel, [jnp.reshape(bit, (1,)).astype(I32)], [],
        [full(turned), row_of(far_pack, 0), row_of(own, 1), row_of(got, 1),
         row_of(pack, 1), row_of(far_pack, 1), row_of(own, 0), row_of(got, 0)],
        [half, half],
        scratch=[VMEM((2, depth, depth), BF16)],
    )


def three_parts(value):
    high = value.astype(BF16)
    rest = value - high.astype(F32)
    middle_part = rest.astype(BF16)
    return high, middle_part, (rest - middle_part.astype(F32)).astype(BF16)


def middle(back, routed, branch, scale2, gate, grad_routed, out_weight, pack, lse, vec):
    width, depth = branch.shape
    tiles = width // TILE
    lots = lse.shape[0]
    extra = -(-lots // 16) * 16

    def kernel(scalars, small, fetches, sends, scratch, scalar_outs):
        back_in, x_in, branch_in, gate_in, grad_in, ow, att, lse_in, vec_in = fetches
        gout, mixed_out, low_out, delta_out, vec_out = sends
        back = back_in()[...]
        unit, inverse = normalize(wide(x_in()) + branch_in()[...])
        vec_out.ref[...] = vec_in()[...]
        vec_out.ref[5:6, :] = jnp.sum(back * unit, axis=0, keepdims=True)
        vec_out.ref[6:7, :] = jnp.sum(back, axis=0, keepdims=True)
        mixed = norm_back(back, wide(small[0]), unit, inverse)
        mixed_out.ref[...] = mixed
        mixed_out.go()
        low = (gate_in()[:, 0:1] * wide(grad_in()) + mixed).astype(BF16)
        low_out.ref[...] = low
        low_out.go()
        vec_out.ref[7:8, :] = jnp.sum(low.astype(F32), axis=0, keepdims=True)
        value = nt(low, ow()[...]).astype(BF16)
        gout.ref[0:width] = value
        product = value.astype(F32) * wide(att())
        high = product.astype(BF16)
        rest = (product - high.astype(F32)).astype(BF16)
        member = lax.broadcasted_iota(I32, (16, depth), 1) // HD
        ones = jnp.where(member == lax.broadcasted_iota(I32, (16, depth), 0), 1.0, 0.0).astype(BF16)
        delta = nt(ones, high) + nt(ones, rest)
        for head in range(H):
            for j in range(tiles):
                lot = (head // 2) * tiles + j
                at = (head % 2) * TILE
                delta_out.ref[lot : lot + 1, at : at + TILE] = delta[head : head + 1, j * TILE : (j + 1) * TILE]
        gout.ref[width:] = jnp.zeros_like(gout.ref[width:])
        for i, part in enumerate(three_parts(lse_in()[...])):
            gout.ref[width : width + lots, i * 2 * TILE : (i + 1) * 2 * TILE] = part
        for i, part in enumerate(three_parts(delta_out.ref[...])):
            gout.ref[width + extra : width + extra + lots, i * 2 * TILE : (i + 1) * 2 * TILE] = part

    low = shape_of((width, depth), BF16)
    return streamed(
        "middle", kernel, [], [scale2],
        [full(back), head_rows(routed, width)]
        + [full(a) for a in (branch, gate, grad_routed, out_weight)] + [row_of(pack, 2)]
        + [full(lse), full(vec)],
        [
            shape_of((width + 2 * extra, depth), BF16),
            shape_of((width, depth), F32),
            low,
            shape_of(lse.shape, F32),
            shape_of((16, depth), F32),
        ],
    )


def own_back(part, parts, q, k, v, gout, lse, delta, fk, fv, lines, spans, far_spans):
    width, depth = q.shape
    tiles = width // TILE
    some = depth // parts
    pairs = some // PAIR
    base = part * pairs * tiles

    def kernel(scalars, small, fetches, sends, scratch, scalar_outs):
        q_in, k_in, v_in, g_in, fk_in, fv_in, lse_in, delta_in, lines_in = fetches
        dq, dk, dv = sends
        bias, far_bias, turned, far_turned, span, far_span, dq_turned = scratch
        lines_ref = lines_in()
        fill_bias(bias, lines_ref[0], lines_ref[0], -1.0)
        fill_bias(far_bias, lines_ref[1], lines_ref[0], -2.0)
        store_spans(span, scalars[0], scalars[0], tiles)
        store_spans(far_span, scalars[1], scalars[0], tiles)
        k_ref, fk_ref, q_ref, g_ref, v_ref, fv_ref = k_in(), fk_in(), q_in(), g_in(), v_in(), fv_in()
        lse_ref, delta_ref = lse_in(), delta_in()
        turned[...] = k_ref[...].T
        far_turned[...] = fk_ref[...].T
        dk.ref[...] = jnp.zeros_like(dk.ref)
        dv.ref[...] = jnp.zeros_like(dv.ref)

        def pieces(j, pair):
            cols = pl.ds(pl.multiple_of(pair * PAIR, PAIR), PAIR)
            rows = pl.ds(pl.multiple_of(j * TILE, TILE), TILE)
            query = stacked_heads(q_ref[rows, cols]) * SCALE
            grad = stacked_heads(g_ref[rows, cols])
            one = pl.ds(base + pair * tiles + j, 1)
            return cols, rows, query, grad, lse_ref[one], delta_ref[one]

        def local(n, j, pair):
            cols, rows, query, grad, top, delta = pieces(j, pair)
            near = pl.ds(pl.multiple_of(span[j] * TILE, TILE), n * TILE)
            weights = jnp.exp(nt(k_ref[near, cols], query) + twice(bias[near, rows]) - top)
            dscore = (weights * (nt(v_ref[near, cols], grad) - delta)).astype(BF16)
            dk.ref[near, cols] += nn(dscore, query)
            dv.ref[near, cols] += nn(weights.astype(BF16), grad)
            dq_turned[cols, rows] = own_blocks(nn(turned[cols, near], dscore))

        def remote(n, j, pair):
            cols, rows, query, grad, top, delta = pieces(j, pair)
            far = pl.ds(pl.multiple_of(far_span[j] * TILE, TILE), n * TILE)
            weights = jnp.exp(nt(fk_ref[far, cols], query) + twice(far_bias[far, rows]) - top)
            dscore = (weights * (nt(fv_ref[far, cols], grad) - delta)).astype(BF16)
            dq_turned[cols, rows] += own_blocks(nn(far_turned[cols, far], dscore))

        over_tiles(span, tiles, pairs, 1, local)
        over_tiles(far_span, tiles, pairs, 1, remote)
        dq.ref[...] = (dq_turned[...].T * SCALE).astype(BF16)

    total = shape_of((width, some), F32)
    return streamed(
        "own_back", kernel, [spans, far_spans], [],
        [columns(a, part * some, some) for a in (q, k, v)]
        + [(gout, lambda ref, scalars: ref.at[0:width, part * some : (part + 1) * some], (width, some))]
        + [columns(a, part * some, some) for a in (fk, fv)]
        + [full(lse), full(delta), full(lines)],
        [shape_of((width, some), BF16), total, total],
        scratch=[
            VMEM((width, width), F32), VMEM((width, width), F32),
            VMEM((some, width), BF16), VMEM((some, width), BF16),
            SMEM((2 * tiles,), I32), SMEM((2 * tiles,), I32), VMEM((some, width), F32),
        ],
    )


def other_back(fgout, core, spans, far_spans, fq, k, v, lines, grads, low, vec):
    width, depth = k.shape
    tiles = width // TILE
    parts = len(grads)
    some = depth // parts
    pairs = some // PAIR
    lots = depth // PAIR * tiles
    extra = -(-lots // 16) * 16
    half = depth // 2

    def kernel(scalars, small, fetches, sends, scratch, scalar_outs):
        g_in, fq_in, k_in, v_in, lines_in, low_in, vec_in = fetches[:7]
        pieces = fetches[7:]
        halves = sends[:4]
        dq, dk, dv, vec_out = sends[4:]
        bias, span, stat, dk_sum, dv_sum = scratch
        lines_ref = lines_in()
        fill_bias(bias, lines_ref[0], lines_ref[1], -1.0)
        store_spans(span, scalars[1], scalars[2], tiles)
        g_ref = g_in()
        for i in range(2):
            block = g_ref[width + i * extra : width + i * extra + lots]
            stat[i] = (
                block[:, 0 : 2 * TILE].astype(F32)
                + block[:, 2 * TILE : 4 * TILE].astype(F32)
                + block[:, 4 * TILE : 6 * TILE].astype(F32)
            )
        fq_ref, k_ref, v_ref = fq_in(), k_in(), v_in()
        for part in range(parts):
            place = slice(part * some, (part + 1) * some)
            dq.ref[:, place] = pieces[3 * part]()[...]
            dk_sum[:, place] = pieces[3 * part + 1]()[...]
            dv_sum[:, place] = pieces[3 * part + 2]()[...]

        def work(n, j, pair):
            cols = pl.ds(pl.multiple_of(pair * PAIR, PAIR), PAIR)
            rows = pl.ds(pl.multiple_of(j * TILE, TILE), TILE)
            one = pl.ds(pair * tiles + j, 1)
            query = stacked_heads(fq_ref[rows, cols]) * SCALE
            grad = stacked_heads(g_ref[rows, cols])
            near = pl.ds(pl.multiple_of(span[j] * TILE, TILE), n * TILE)
            scores = nt(k_ref[near, cols], query) + twice(bias[near, rows])
            weights = jnp.exp(scores - stat[0, one])
            dscore = (weights * (nt(v_ref[near, cols], grad) - stat[1, one])).astype(BF16)
            dk_sum[near, cols] += nn(dscore, query)
            dv_sum[near, cols] += nn(weights.astype(BF16), grad)

        over_tiles(span, tiles, depth // PAIR, 1, work)
        dk.ref[...] = dk_sum[...].astype(BF16)
        dv.ref[...] = dv_sum[...].astype(BF16)
        low_ref = low_in()
        cols = pl.ds(pl.multiple_of((1 - scalars[0][0]) * half, TILE), half)
        for out, ref in zip(halves, (dq.ref, dk.ref, dv.ref, low_ref)):
            out.ref[...] = ref[:, cols]
            out.go()
        vec_out.ref[...] = vec_in()[...]
        vec_out.ref[8:9, :] = jnp.sum(wide(dq.ref), axis=0, keepdims=True)
        vec_out.ref[9:10, :] = jnp.sum(wide(dv.ref), axis=0, keepdims=True)

    flat = [piece for grad in grads for piece in grad]
    low_shape = shape_of((width, depth), BF16)
    return streamed(
        "other_back", kernel, [core, spans, far_spans], [],
        [full(a) for a in (fgout, fq, k, v, lines, low, vec)] + [full(a) for a in flat],
        [shape_of((width, half), BF16)] * 4 + [low_shape] * 3 + [shape_of((16, depth), F32)],
        scratch=[
            VMEM((width, width), F32), SMEM((2 * tiles,), I32), VMEM((2, lots, 2 * TILE), F32),
            VMEM((width, depth), F32), VMEM((width, depth), F32),
        ],
    )


def last_grads(core, bit, pack, far_pack, dq, dk, dv, low, got):
    width, depth = dq.shape
    half = depth // 2

    def kernel(scalars, small, fetches, sends, scratch, scalar_outs):
        normed, far_normed, att, far_att, dq_in, dk_in, dv_in, low_in = fetches[:8]
        gots = fetches[8:]
        send, keep = sends
        turned = scratch[0]
        cols = pl.ds(pl.multiple_of(scalars[0][0] * half, TILE), half)
        for i, ref in enumerate((normed, far_normed, att, far_att)):
            turned[i // 2, :, (i % 2) * width : (i % 2 + 1) * width] = ref()[...].T
        for out, which in ((send, 1 - scalars[1][0]), (keep, scalars[1][0])):
            rows = pl.ds(pl.multiple_of(which * half, TILE), half)
            for i, part in enumerate((dq_in, dk_in, dv_in, low_in)):
                place = slice(i * half, (i + 1) * half)
                side = 0 if i < 3 else 1
                value = nn(turned[side, rows, 0:width], part()[:, cols])
                value = value + nn(turned[side, rows, width : 2 * width], gots[i]()[...])
                out.ref[:, place] = value.astype(BF16)
            out.go()

    shape = shape_of((half, 2 * depth), BF16)
    return streamed(
        "last_grads", kernel, [core, jnp.reshape(bit, (1,)).astype(I32)], [],
        [row_of(pack, 3), row_of(far_pack, 3), row_of(pack, 2), row_of(far_pack, 2)]
        + [full(a) for a in (dq, dk, dv, low) + tuple(got)],
        [shape, shape],
        scratch=[VMEM((2, depth, 2 * width), BF16)],
    )


def scatter(hot_ref, rows, slots_ref):
    hot = hot_ref[...]
    taken = jnp.max(hot.astype(F32), axis=-1, keepdims=True) > 0.0
    return jnp.where(taken, nn(hot, rows).astype(BF16), slots_ref[...])


def token_out(hot, tokens, routed, gate, branch, feed, down_bias, grad_routed, router, mixed, vec):
    slots, depth = tokens.shape
    width = branch.shape[0]

    def kernel(scalars, small, fetches, sends, scratch, scalar_outs):
        branch_in, feed_in, x_in, gate_in, grad_in, mixed_in, vec_in, hot_in, tok_in = fetches
        out, base, vec_out = sends
        total = branch_in()[...] + feed_in()[...] + wide(small[0])
        x = wide(x_in())
        gate = gate_in()[:, 0:1]
        grad = wide(grad_in())
        logit = jnp.sum(grad * total, axis=-1, keepdims=True) * gate * (1.0 - gate)
        base.ref[...] = grad + mixed_in()[...] + logit * wide(small[1])
        base.go()
        vec_out.ref[...] = vec_in()[...]
        vec_out.ref[12:13, :] = jnp.sum(x * logit, axis=0, keepdims=True)
        out.ref[...] = scatter(hot_in(), (x + gate * total).astype(BF16), tok_in())

    return streamed(
        "token_out", kernel, [], [down_bias, router],
        [full(branch), full(feed), head_rows(routed, width)]
        + [full(a) for a in (gate, grad_routed, mixed, vec, hot, tokens)],
        [shape_of((slots, depth), BF16), shape_of((width, depth), F32), shape_of((16, depth), F32)],
    )


def token_grad(dq, dk, dv, hot, cotangent, routed, base, scale, qkv_weight, vec):
    slots, depth = cotangent.shape
    width = base.shape[0]

    def kernel(scalars, small, fetches, sends, scratch, scalar_outs):
        dq_in, weight_q, dk_in, weight_k, dv_in, weight_v, x_in, base_in, vec_in, hot_in, cot_in = fetches
        out, vec_out = sends
        back = nt(dq_in()[...], weight_q()[...]) + nt(dk_in()[...], weight_k()[...])
        back = back + nt(dv_in()[...], weight_v()[...])
        unit, inverse = normalize(wide(x_in()))
        vec_out.ref[...] = vec_in()[...]
        vec_out.ref[10:11, :] = jnp.sum(back * unit, axis=0, keepdims=True)
        vec_out.ref[11:12, :] = jnp.sum(back, axis=0, keepdims=True)
        vec_out.go()
        rows = (base_in()[...] + norm_back(back, wide(small[0]), unit, inverse)).astype(BF16)
        out.ref[...] = scatter(hot_in(), rows, cot_in())

    return streamed(
        "token_grad", kernel, [], [scale],
        [
            full(dq), columns(qkv_weight, 0, depth), full(dk), columns(qkv_weight, depth, depth),
            full(dv), columns(qkv_weight, 2 * depth, depth), head_rows(routed, width),
            full(base), full(vec), full(hot), full(cotangent),
        ],
        [shape_of((slots, depth), BF16), shape_of((16, depth), F32)],
    )


AXES = ("rows", "seq")
SHIFT = {"c": 0, "x": 1, "z1": 2, "z2": 3}
BLOCK = 16
XY_FIRST = (("x", "y"), ("y", "x"), ("z1", "z1"), ("z2", "z2"))
Z_FIRST = (("z1", "z1"), ("x", "y"), ("y", "x"), ("z2", "z2"))
X_FIRST = (("x", "x"), ("y", "y"), ("z1", "z1"), ("z2", "z2"))


def swap(block, axes):
    route = []
    for row in range(lax.axis_size("rows")):
        axis = axes[row & 1]
        for seq in range(2):
            if axis == "y":
                other = row * 2 + (seq ^ 1)
            else:
                other = (row ^ (1 << SHIFT[axis])) * 2 + seq
            route.append((row * 2 + seq, other))
    return lax.ppermute(block, AXES, route)


def own_bit(axis):
    if axis == "y":
        return lax.axis_index("seq")
    return (lax.axis_index("rows") >> SHIFT[axis]) & 1


def stage_bit(axes, core):
    if axes[0] == axes[1]:
        return own_bit(axes[0])
    return jnp.where(core == 0, own_bit(axes[0]), own_bit(axes[1]))


def half_of(block, which):
    half = block.shape[0] // 2
    return lax.dynamic_slice_in_dim(block, which * half, half, 0)


def add_low(left, right):
    return (left.astype(F32) + right.astype(F32)).astype(BF16)


def after(value, *others):
    return lax.optimization_barrier((value, *others))[0]


def over_blocks(total):
    extra = BLOCK
    size = lax.axis_size("rows")
    while extra < size:
        route = [(i * 2 + j, (i ^ extra) * 2 + j) for i in range(size) for j in range(2)]
        got = lax.ppermute(total, AXES, route)
        total = (total.astype(F32) + got.astype(F32)).astype(total.dtype)
        extra *= 2
    return total


class Order:
    def __init__(self):
        self.tail = None

    def run(self, call, lead, *args):
        if self.tail is not None:
            lead = after(lead, self.tail)
        result = call(lead, *args)
        self.tail = jax.tree.leaves(result)[-1]
        return result


class Sum:
    def __init__(self, order, send, keep, stages):
        self.order, self.keep, self.stages, self.at = order, keep, stages, 1
        self.got = swap(send, stages[0])

    def reduce(self):
        if self.at == len(self.stages):
            self.keep = over_blocks(self.order.run(add_low, self.got, self.keep))
            self.got = swap(self.keep, self.stages[-1])
            return
        axes = self.stages[self.at]
        bit = stage_bit(axes, own_bit("c"))
        send = self.order.run(lambda got, keep: add_low(half_of(keep, 1 - bit), half_of(got, 1 - bit)), self.got, self.keep)
        got = swap(send, axes)
        self.keep = self.order.run(lambda got, keep: add_low(half_of(keep, bit), half_of(got, bit)), self.got, self.keep)
        self.got = got
        self.at += 1

    def gather(self):
        self.at -= 1
        self.keep = self.order.run(lambda got, keep: jnp.concatenate([keep, got]), self.got, self.keep)
        self.got = swap(self.keep, self.stages[self.at - 1] if self.at else ("c", "c"))


class SmallSum:
    def __init__(self, order, block):
        self.order, self.block, self.left = order, block, ["c", "x", "y", "z1", "z2"]
        self.send()

    def send(self):
        axis = self.left.pop(0)
        self.got = swap(self.block, (axis, axis))

    def step(self):
        self.block = self.order.run(lambda got, block: got + block, self.got, self.block)
        if self.left:
            self.send()

    def total(self):
        return over_blocks(self.block)


def shard_of(stages, core):
    index = jnp.int32(0)
    for axes in stages:
        index = index * 2 + stage_bit(axes, core)
    return index


SHARDS = 16


def place_kernel(split, info_ref, block_ref, *rest):
    first_ref, second_ref, low, full, sems = rest[-5:]
    rows = block_ref.shape[0] // SHARDS
    own = info_ref[0]
    lot = info_ref[1]
    depth = block_ref.shape[1]

    def pull(s):
        src = pl.ds(pl.multiple_of((s ^ own) * rows, rows), rows)
        dst = pl.ds(s * rows, rows)
        return pltpu.make_async_copy(block_ref.at[src], low.at[dst], sems.at[0, s])

    def push(s):
        src = pl.ds(s * rows, rows)
        if split == "feed":
            per = SHARDS // 2
            if s < per:
                to = first_ref.at[pl.ds(s * rows, rows), pl.ds(pl.multiple_of(lot * depth, 128), depth)]
            else:
                to = second_ref.at[pl.ds(pl.multiple_of(lot * depth + (s - per) * rows, rows), rows)]
            return [pltpu.make_async_copy(full.at[src], to, sems.at[1, s])]
        part = depth // 4
        copies = []
        for t in range(4):
            target = first_ref if t < 3 else second_ref
            at = (2 * t + lot) * part if t < 3 else lot * part
            copies.append(
                pltpu.make_async_copy(
                    full.at[src, pl.ds(t * part, part)],
                    target.at[pl.ds(s * rows, rows), pl.ds(pl.multiple_of(at, 128), part)],
                    sems.at[1 + t, s],
                )
            )
        return copies

    for s in range(SHARDS):
        pull(s).start()
    for s in range(SHARDS):
        pull(s).wait()
        dst = slice(s * rows, (s + 1) * rows)
        full[dst] = low[dst].astype(F32)
        for copy in push(s):
            copy.start()
    for s in range(SHARDS):
        for copy in push(s):
            copy.wait()


def place(split, info, block, targets, shapes):
    hbm = pl.BlockSpec(memory_space=pl.ANY)
    targets = targets or ()
    return pl.pallas_call(
        functools.partial(place_kernel, split),
        out_shape=tuple(jax.ShapeDtypeStruct(s, F32) for s in shapes),
        in_specs=[pl.BlockSpec(memory_space=pltpu.SMEM), hbm] + [hbm] * len(targets),
        out_specs=(hbm, hbm),
        scratch_shapes=[
            VMEM(block.shape, BF16),
            VMEM(block.shape, F32),
            pltpu.SemaphoreType.DMA((5, SHARDS)),
        ],
        input_output_aliases={2: 0, 3: 1} if targets else {},
        compiler_params=pltpu.CompilerParams(vmem_limit_bytes=16 << 20),
        cost_estimate=pl.CostEstimate(flops=0, bytes_accessed=0, transcendentals=0),
        name="place",
    )(info, block, *targets)


def body(
    tokens,
    cotangent,
    segment_ids,
    routing,
    qkv_weight,
    query_bias,
    value_bias,
    out_weight,
    out_bias,
    first_scale,
    first_offset,
    second_scale,
    second_offset,
    up_weight,
    up_bias,
    down_weight,
    down_bias,
    router_weight,
):
    row_count, slots, depth = tokens.shape
    hidden = up_weight.shape[1]
    count = slots // 2
    width = -(-count // 128) * 128
    core = own_bit("c")
    seat = jnp.reshape(core, (1,)).astype(jnp.int32)
    pos = jnp.reshape(lax.axis_index("seq"), (1,)).astype(jnp.int32)
    tokens = tokens.reshape(slots, depth)
    cotangent = cotangent.reshape(slots, depth)
    routes = routing.reshape(2, 1, slots)
    segs = segment_ids.reshape(2, 1, slots)
    qb, vb, ob, s1, o1, s2, o2, db, rw = (
        v.reshape(1, depth)
        for v in (query_bias, value_bias, out_bias, first_scale, first_offset, second_scale,
                  second_offset, down_bias, router_weight)
    )
    ub = up_bias.reshape(1, hidden)

    order = Order()
    routed, grad_routed, hot, spans = pick_rows(pos, routes, segs, tokens, cotangent, count, width)
    far = swap(routed, ("y", "y"))
    q, k, v, normed, gate, acc, stat = near_attention(spans, routed, qkv_weight, qb, vb, s1, o1, rw)
    fq, fk, fv, pack, lse, branch, turned, lines, far_spans = order.run(
        far_attention, far, spans, routed, qkv_weight, qb, vb, s1, o1, count, q, acc, stat,
        out_weight, ob, s2, o2, gate, grad_routed, normed
    )
    far_pack = swap(pack, ("c", "c"))

    plans = (Z_FIRST, X_FIRST, XY_FIRST)
    first_bits = [stage_bit(plan[0], core) for plan in plans]
    gots, owns = [], []
    carried = None
    for pair in range(2):
        send, own, *carried = order.run(feed_blocks, seat, pack, up_weight, ub, down_weight, carried, pair)
        gots.append(swap(send, ("c", "c")))
        owns.append(own)
    back, feed_sum, vec = carried

    def feed_sums(pair):
        send, keep = order.run(
            feed_grads, gots[pair], first_bits[pair], turned, pack, far_pack, owns[pair]
        )
        return Sum(order, send, keep, plans[pair])

    one = feed_sums(0)
    two = feed_sums(1)
    gout, mixed, low, delta, vec = order.run(
        middle, back, routed, branch, s2, gate, grad_routed, out_weight, pack, lse, vec
    )
    fgout = swap(gout, ("y", "y"))
    grads = [
        order.run(
            lambda q, part=part: own_back(part, 2, q, k, v, gout, lse, delta, fk, fv, lines, spans, far_spans), q
        )
        for part in range(2)
    ]
    one.reduce()
    out_tokens, base, vec = order.run(
        token_out, hot, tokens, routed, gate, branch, feed_sum, db, grad_routed, rw, mixed, vec
    )
    two.reduce()
    *last_sends, dq, dk, dv, vec = order.run(
        other_back, fgout, seat, spans, far_spans, fq, k, v, lines, grads, low, vec
    )
    gots = [swap(send, ("c", "c")) for send in last_sends]
    one.reduce()
    two.reduce()
    grad_tokens, vec = order.run(token_grad, dq, dk, dv, hot, cotangent, routed, base, s1, qkv_weight, vec)
    one.reduce()
    two.reduce()
    send, keep = order.run(
        lambda got, *rest: last_grads(seat, first_bits[2], pack, far_pack, dq, dk, dv, low, (got,) + rest), *gots
    )
    three = Sum(order, send, keep, plans[2])
    small = SmallSum(order, vec)
    one.reduce()
    two.reduce()
    three.reduce()
    small.step()
    one.gather()
    two.gather()
    three.reduce()
    small.step()
    one.gather()
    two.gather()
    three.reduce()
    small.step()
    one.gather()
    two.gather()
    three.reduce()
    small.step()
    three.gather()
    small.step()
    three.gather()
    one.gather()
    two.gather()
    three.gather()
    vec = small.total()

    def put(part, index, targets):
        plan = plans[index]
        shapes, kind = ((depth, hidden), (hidden, depth)), "feed"
        if index == 2:
            shapes, kind = ((depth, 3 * depth), (depth, depth)), "last"
        for block, owner in ((part.keep, core), (part.got, 1 - core)):
            lot = owner if index == 2 else 2 * index + owner
            info = jnp.stack([shard_of(plan, owner), lot]).astype(jnp.int32)
            targets = order.run(lambda info, *rest: place(kind, info, *rest), info, block, targets, shapes)
        return targets

    pair_grads = put(one, 0, None)
    three.gather()
    grad_qkv, grad_out = put(three, 2, None)
    grad_up, grad_down = put(two, 1, pair_grads)
    return (
        out_tokens.reshape(row_count, slots, depth),
        grad_tokens.reshape(row_count, slots, depth),
        grad_qkv,
        vec[8],
        vec[9],
        grad_out,
        vec[7],
        vec[10],
        vec[11],
        vec[5],
        vec[6],
        grad_up,
        vec[0:4].reshape(hidden),
        grad_down,
        vec[4],
        vec[12],
    )


def solution(mesh):
    split = P("rows", "seq", None)
    return jax.shard_map(
        body,
        mesh=mesh,
        in_specs=(split, split, P("rows", None), P("rows", None)) + (P(),) * 14,
        out_specs=(split, split) + (P(),) * 14,
        check_vma=False,
    )
```

```python
import functools

import jax
import jax.numpy as jnp
from jax import lax
from jax.experimental import pallas as pl
from jax.experimental.pallas import tpu as pltpu
from jax.sharding import PartitionSpec as P

H = 12
HD = 64
PAIR = 2 * HD
TILE = 128
NEG = -1e30
SCALE = HD ** (-0.5)
RATE = 1.15e9
LENGTH = {
    "pick_rows": 6.0,
    "near_attention": 14.0,
    "far_and_feed": 36.0,
    "feed_grads": 3.0,
    "own_back": 5.0,
    "other_back": 1.0,
    "token_out": 1.0,
    "last_grads": 8.0,
    "token_grad": 14.0,
    "place": 1.0,
}
F32 = jnp.float32
BF16 = jnp.bfloat16
I32 = jnp.int32
VMEM = pltpu.VMEM
SMEM = pltpu.SMEM


def nn(a, b):
    return lax.dot_general(a, b, (((1,), (0,)), ((), ())), preferred_element_type=F32)


def nt(a, b):
    return lax.dot_general(a, b, (((1,), (1,)), ((), ())), preferred_element_type=F32)


def tn(a, b):
    return lax.dot_general(a, b, (((0,), (0,)), ((), ())), preferred_element_type=F32)


def shape_of(shape, kind):
    return jax.ShapeDtypeStruct(shape, kind)


class Fetch:
    def __init__(self, copies, target):
        self.copies, self.target = copies, target
        self.waiting = set(range(len(copies)))
        for copy in copies:
            copy.start()

    def __call__(self, piece=None):
        for i in sorted(self.waiting) if piece is None else [piece]:
            if i in self.waiting:
                self.copies[i].wait()
                self.waiting.discard(i)
        return self.target


class Send:
    def __init__(self, buffer, target, sems, pieces):
        self.ref, self.target, self.sem, self.copies = buffer, target, sems, []
        for i in range(pieces):
            source, to = (buffer, target) if pieces == 1 else (buffer.at[i], target.at[i])
            self.copies.append(pltpu.make_async_copy(source, to, sems.at[i]))
        self.left = set(range(pieces))

    def go(self, piece=None):
        for i in sorted(self.left) if piece is None else [piece]:
            if i in self.left:
                self.copies[i].start()
                self.left.discard(i)

    def wait(self):
        self.go()
        for copy in self.copies:
            copy.wait()


def streamed(name, kernel, scalars, small, large, outs, scratch=(), scalar_outs=(), room=62, split=()):
    arrays, plans = [], []
    for array, parts, extent in large:
        at = next((i for i, a in enumerate(arrays) if a is array), None)
        if at is None:
            at = len(arrays)
            arrays.append(array)
        if parts is None or callable(parts):
            parts = [(parts, None)]
        plans.append((at, parts, extent))
    most_in = max(len(p) for _, p, _ in plans)
    counts = [o.shape[0] if i in split else 1 for i, o in enumerate(outs)]

    def wrapped(*refs):
        refs = list(refs)

        def take(count):
            head = refs[:count]
            del refs[:count]
            return head

        scalar_refs = take(len(scalars))
        small_refs = take(len(small))
        array_refs = take(len(arrays))
        out_refs = take(len(outs))
        scalar_out_refs = take(len(scalar_outs))
        landing = take(len(plans))
        staging = take(len(outs))
        in_sems, out_sems = take(2)
        fetches = []
        for i, (at, parts, _) in enumerate(plans):
            copies = []
            for j, (source, place) in enumerate(parts):
                start = array_refs[at] if source is None else source(array_refs[at], scalar_refs)
                to = landing[i] if place is None else place(landing[i])
                copies.append(pltpu.make_async_copy(start, to, in_sems.at[i, j]))
            fetches.append(Fetch(copies, landing[i]))
        sends = [Send(staging[i], out_refs[i], out_sems.at[i], counts[i]) for i in range(len(outs))]
        kernel(scalar_refs, small_refs, fetches, sends, refs, scalar_out_refs)
        for fetch in fetches:
            fetch()
        for send in sends:
            send.go()
        for send in sends:
            send.wait()

    hbm = pl.BlockSpec(memory_space=pltpu.HBM)
    return pl.pallas_call(
        wrapped,
        out_shape=tuple(outs) + tuple(scalar_outs),
        in_specs=[pl.BlockSpec(memory_space=SMEM)] * len(scalars)
        + [pl.BlockSpec(memory_space=VMEM)] * len(small)
        + [hbm] * len(arrays),
        out_specs=tuple([hbm] * len(outs) + [pl.BlockSpec(memory_space=SMEM)] * len(scalar_outs)),
        scratch_shapes=[VMEM(extent, arrays[at].dtype) for at, _, extent in plans]
        + [VMEM(o.shape, o.dtype) for o in outs]
        + [pltpu.SemaphoreType.DMA((len(plans), most_in)), pltpu.SemaphoreType.DMA((len(outs), max(counts)))]
        + list(scratch),
        compiler_params=pltpu.CompilerParams(vmem_limit_bytes=room << 20),
        cost_estimate=pl.CostEstimate(flops=int(LENGTH[name] * RATE), bytes_accessed=0, transcendentals=0),
        name=name,
    )(*scalars, *small, *arrays)


def full(array):
    return (array, None, array.shape)


def row_of(array, index):
    return (array, lambda ref, scalars: ref.at[index], array.shape[1:])


def head_rows(array, count):
    return (array, lambda ref, scalars: ref.at[0:count], (count,) + array.shape[1:])


def columns(array, start, count):
    return (array, lambda ref, scalars: ref.at[:, start : start + count], (array.shape[0], count))


def wide(ref):
    return ref[...].astype(F32)


def normalize(values):
    center = values - jnp.mean(values, axis=-1, keepdims=True)
    inverse = lax.rsqrt(jnp.mean(center * center, axis=-1, keepdims=True) + 1e-06)
    return center * inverse, inverse


def norm_back(grad, scale, unit, inverse):
    scaled = grad * scale
    first = jnp.mean(scaled, axis=-1, keepdims=True)
    second = jnp.mean(scaled * unit, axis=-1, keepdims=True)
    return inverse * (scaled - first - unit * second)


def tile_spans(line, count, out_ref):
    width = line.shape[1]
    lane = lax.broadcasted_iota(I32, (1, width), 1)
    tiles = width // TILE
    for i in range(tiles):
        inside = (lane >= i * TILE) & (lane < min((i + 1) * TILE, count))
        out_ref[i] = jnp.min(jnp.where(inside, line, 1e9)).astype(I32)
        out_ref[tiles + i] = jnp.max(jnp.where(inside, line, -1e9)).astype(I32)


def pick_rows(pos, routes, segs, tokens, cotangent, count, width):
    slots, depth = tokens.shape

    def kernel(scalars, small, fetches, sends, scratch, scalar_outs):
        route, seg, tok, cot = fetches
        routed, grad, hot_out = sends
        lane = lax.broadcasted_iota(I32, (slots, width), 1)
        slot = lax.broadcasted_iota(I32, (slots, width), 0)
        chosen = (slot == route()[:, :width]) & (lane < count)
        taken = jnp.max(jnp.where(chosen, 1.0, 0.0), axis=-1, keepdims=True)
        before = lax.broadcasted_iota(I32, (slots, slots), 0) < lax.broadcasted_iota(I32, (slots, slots), 1)
        before = jnp.where(before, 1.0, 0.0).astype(BF16)
        rank = tn(before, jnp.broadcast_to(taken, (slots, TILE)).astype(BF16))[:, 0:1]
        rank = jnp.where(taken > 0.0, rank, -1.0)
        hot = jnp.where(lane.astype(F32) == rank, 1.0, 0.0).astype(BF16)
        hot_out.ref[...] = hot
        hot_out.go()
        groups = jnp.broadcast_to(seg()[...].astype(F32), (8, slots)).astype(BF16)
        line = nn(groups, hot)
        line = jnp.where(lax.broadcasted_iota(I32, (8, width), 1) < count, line, -1.0)
        routed.ref[0:width] = tn(hot, tok()[...]).astype(BF16)
        routed.ref[width:] = jnp.zeros_like(routed.ref[width:])
        routed.ref[width : width + 8, 0:width] = line.astype(BF16)
        routed.go()
        grad.ref[...] = tn(hot, cot()[...]).astype(BF16)
        tile_spans(line[0:1], count, scalar_outs[0])

    return streamed(
        "pick_rows", kernel, [pos], [],
        [
            (routes, lambda ref, scalars: ref.at[scalars[0][0]], routes.shape[1:]),
            (segs, lambda ref, scalars: ref.at[scalars[0][0]], segs.shape[1:]),
            full(tokens), full(cotangent),
        ],
        [shape_of((width + 16, depth), BF16), shape_of((width, depth), BF16), shape_of((slots, width), BF16)],
        scalar_outs=[shape_of((2 * (width // TILE),), I32)],
    )


def key_span(keys, queries, j, tiles):
    low, high = queries[j], queries[tiles + j]
    first, last = jnp.int32(tiles), jnp.int32(-1)
    for t in range(tiles):
        meets = (keys[tiles + t] >= low) & (keys[t] <= high)
        first = jnp.where(meets & (first == tiles), t, first)
        last = jnp.where(meets, t, last)
    return jnp.minimum(first, tiles - 1), jnp.maximum(last - first + 1, 0)


def store_spans(ref, keys, queries, tiles):
    for j in range(tiles):
        first, many = key_span(keys, queries, j, tiles)
        ref[j] = first
        ref[tiles + j] = many


def fill_bias(bias_ref, key_line, query_line, key_pad):
    keys = jnp.where(key_line < 0.0, key_pad, key_line).T[:, 0:1]
    bias_ref[...] = jnp.where(keys == query_line[0:1], 0.0, NEG)


def fill_row_bias(bias_ref, key_line, query_line, key_pad):
    keys = jnp.where(key_line < 0.0, key_pad, key_line)[0:1]
    bias_ref[...] = jnp.where(query_line.T[:, 0:1] == keys, 0.0, NEG)


def first_head():
    return lax.broadcasted_iota(I32, (1, PAIR), 1) < HD


def attend_rows(query, keys, values, bias):
    first = first_head()
    zero = jnp.zeros_like(query)
    wide_values = jnp.concatenate([values, jnp.ones_like(values)], axis=1)
    sums, tops = [], []
    for head in range(2):
        some = jnp.where(first if head == 0 else jnp.logical_not(first), query, zero) * SCALE
        scores = nt(some, keys) + bias
        top = jnp.max(scores, axis=1, keepdims=True)
        sums.append(nn(jnp.exp(scores - top).astype(BF16), wide_values))
        tops.append(top)
    value = jnp.where(first, sums[0][:, 0:PAIR], sums[1][:, 0:PAIR])
    total = jnp.where(first, sums[0][:, PAIR:], sums[1][:, PAIR:])
    return value, total, jnp.where(first, tops[0], tops[1])


def stacked_heads(block):
    lane = lax.broadcasted_iota(I32, (1, PAIR), 1)
    zero = jnp.zeros_like(block)
    return jnp.concatenate([jnp.where(lane < HD, block, zero), jnp.where(lane >= HD, block, zero)], axis=0)


def own_blocks(block):
    return jnp.concatenate([block[0:HD, 0:TILE], block[HD:PAIR, TILE : 2 * TILE]], axis=0)


def twice(block):
    return jnp.concatenate([block, block], axis=1)


def over_tiles(span, tiles, pairs, lowest, work, group=3):
    def tile_step(j, carry):
        for n in range(lowest, tiles + 1):

            def branch(n=n):
                def group_step(i, inner):
                    for p in range(group):
                        work(n, j, i * group + p)
                    return inner

                lax.fori_loop(0, pairs // group, group_step, 0)

            pl.when(span[tiles + j] == n)(branch)
        return carry

    lax.fori_loop(0, tiles, tile_step, 0)


def project(normed, weights, qb, vb, q_ref, k_ref, v_ref, sends):
    depth = normed.shape[1]
    step = 256
    for part, (ref, weight) in enumerate(zip((k_ref, q_ref, v_ref), (weights[1], weights[0], weights[2]))):
        weight_ref = weight()
        for at in range(0, depth, step):
            value = nn(normed, weight_ref[:, at : at + step])
            if part == 1:
                value = value + qb[:, at : at + step]
            elif part == 2:
                value = value + vb[:, at : at + step]
            ref[:, at : at + step] = value.astype(BF16)
        sends[part].go()


def near_attention(spans, routed, qkv_weight, query_bias, value_bias, scale, offset, router):
    depth = routed.shape[1]
    width = routed.shape[0] - 16
    tiles = width // TILE
    pairs = depth // PAIR

    def kernel(scalars, small, fetches, sends, scratch, scalar_outs):
        qb, vb, scale_ref, offset_ref, router_ref = small
        q, k, v, normed, gate, acc, lse = sends
        bias, span = scratch
        x_ref = fetches[0]()
        x = x_ref[0:width].astype(F32)
        unit, _ = normalize(x)
        low = (unit * wide(scale_ref) + wide(offset_ref)).astype(BF16)
        normed.ref[...] = low
        normed.go()
        project(low, fetches[1:4], wide(qb), wide(vb), q.ref, k.ref, v.ref, (k, q, v))
        logit = jnp.sum(x * wide(router_ref), axis=-1, keepdims=True)
        gate.ref[...] = jnp.broadcast_to(1.0 / (1.0 + jnp.exp(-logit)), gate.ref.shape)
        gate.go()
        line = x_ref[width : width + 8, 0:width].astype(F32)
        fill_row_bias(bias, line, line, -1.0)
        store_spans(span, scalars[0], scalars[0], tiles)

        def work(n, j, pair):
            cols = pl.ds(pl.multiple_of(pair * PAIR, PAIR), PAIR)
            rows = pl.ds(pl.multiple_of(j * TILE, TILE), TILE)
            some = pl.ds(pl.multiple_of(span[j] * TILE, TILE), n * TILE)
            value, total, top = attend_rows(q.ref[rows, cols], k.ref[some, cols], v.ref[some, cols], bias[rows, some])
            acc.ref[rows, cols] = value / total
            lse.ref[rows, cols] = top + jnp.log(total)

        over_tiles(span, tiles, pairs, 1, work)

    low = shape_of((width, depth), BF16)
    total = shape_of((width, depth), F32)
    return streamed(
        "near_attention", kernel, [spans], [query_bias, value_bias, scale, offset, router],
        [full(routed)] + [columns(qkv_weight, i * depth, depth) for i in range(3)],
        [low, low, low, low, shape_of((width, TILE), F32), total, total],
        scratch=[VMEM((width, width), F32), SMEM((2 * tiles,), I32)],
    )


def three_parts(value):
    high = value.astype(BF16)
    rest = value - high.astype(F32)
    middle_part = rest.astype(BF16)
    return high, middle_part, (rest - middle_part.astype(F32)).astype(BF16)


def far_and_feed(far, spans, core, routed, qkv_weight, query_bias, value_bias, scale, offset, count,
                 queries, acc, near_lse, out_weight, out_bias, scale2, offset2, gate, grad_routed,
                 up_weight, up_bias, down_weight):
    depth = routed.shape[1]
    width = routed.shape[0] - 16
    tiles = width // TILE
    pairs = depth // PAIR
    lots = pairs * tiles
    extra = -(-lots // 16) * 16
    step = 256
    steps = depth // step
    blocks = up_weight.shape[1] // depth

    def block_of(at, scalars):
        own = scalars[1][0]
        return at // 2 * 2 + (1 - own if at % 2 == 0 else own)

    def up_part(at):
        def piece(i):
            def source(ref, scalars):
                start = pl.multiple_of(block_of(at, scalars) * depth + i * step, step)
                return ref.at[:, pl.ds(start, step)]
            return source, lambda ref: ref.at[:, i * step : (i + 1) * step]
        return (up_weight, [piece(i) for i in range(steps)], (depth, depth))

    def down_part(at):
        def part(ref, scalars):
            return ref.at[pl.ds(pl.multiple_of(block_of(at, scalars) * depth, step), depth)]
        return (down_weight, part, (depth, depth))

    def kernel(scalars, small, fetches, sends, scratch, scalar_outs):
        qb, vb, scale_ref, offset_ref, ob, scale2_ref, offset2_ref, ub = small
        far_in, weight_q, weight_k, weight_v, x_in, q_in, acc_in, lse_in, gate_in, grad_in, ow = fetches[:11]
        ups, downs = fetches[11::2], fetches[12::2]
        fq, fk, fv, pack, lse, branch_out, lines = sends[:7]
        acts = sends[7 : 7 + blocks]
        feed_out, gout, mixed_out, low_out, delta_out, vec_out = sends[7 + blocks :]
        bias, span, attended, back = scratch
        far_ref = far_in()
        far_line = far_ref[width : width + 8, 0:width].astype(F32)
        tile_spans(far_line[0:1], count, scalar_outs[0])
        unit, _ = normalize(far_ref[0:width].astype(F32))
        low = (unit * wide(scale_ref) + wide(offset_ref)).astype(BF16)
        project(low, (weight_q, weight_k, weight_v), wide(qb), wide(vb), fq.ref, fk.ref, fv.ref, (fk, fq, fv))
        x_ref = x_in()
        line = x_ref[width : width + 8, 0:width].astype(F32)
        fill_row_bias(bias, far_line, line, -2.0)
        lines.ref[0] = line
        lines.ref[1] = jnp.where(far_line < 0.0, -2.0, far_line)
        lines.go()
        grad_delta = gate_in()[:, 0:1] * wide(grad_in())
        pack.ref[1] = grad_delta.astype(BF16)
        pack.go(1)
        vec_out.ref[...] = jnp.zeros_like(vec_out.ref)
        vec_out.ref[4:5, :] = jnp.sum(wide(pack.ref.at[1]), axis=0, keepdims=True)
        store_spans(span, scalar_outs[0], scalars[0], tiles)
        q_ref, acc_ref, lse_ref = q_in(), acc_in(), lse_in()

        def work(n, j, pair):
            cols = pl.ds(pl.multiple_of(pair * PAIR, PAIR), PAIR)
            rows = pl.ds(pl.multiple_of(j * TILE, TILE), TILE)
            part, log_total = acc_ref[rows, cols], lse_ref[rows, cols]
            if n > 0:
                some = pl.ds(pl.multiple_of(span[j] * TILE, TILE), n * TILE)
                value, total, top = attend_rows(
                    q_ref[rows, cols], fk.ref[some, cols], fv.ref[some, cols], bias[rows, some]
                )
                most = jnp.maximum(top, log_total)
                far_part = jnp.exp(top - most)
                near_part = jnp.exp(log_total - most)
                total = far_part * total + near_part
                part = (part * near_part + value * far_part) / total
                log_total = most + jnp.log(total)
            attended[rows, cols] = part.astype(BF16)
            turned = log_total.T
            lse.ref[pl.ds(pair * tiles + j, 1)] = jnp.concatenate([turned[0:1], turned[HD : HD + 1]], axis=1)

        over_tiles(span, tiles, pairs, 0, work)
        pack.ref[2] = attended[...]
        pack.go(2)
        branch = nn(attended[...], ow()[...]) + wide(ob)
        branch_out.ref[...] = branch
        branch_out.go()
        unit, _ = normalize(x_ref[0:width].astype(F32) + branch)
        pack.ref[0] = (unit * wide(scale2_ref) + wide(offset2_ref)).astype(BF16)
        pack.go(0)

        second, gfl = pack.ref.at[0], pack.ref.at[1]
        for at, out in enumerate(acts):
            block = block_of(at, scalars)
            for i in range(steps):
                cols = slice(i * step, (i + 1) * step)
                start = pl.multiple_of(block * depth + i * step, step)
                pre = nn(second[...], ups[at](i)[:, cols])
                pre = pre + ub[:, pl.ds(start, step)].astype(F32)
                squared = pre * pre
                inner = pre * (0.7978845608028654 + 0.035677408136300125 * squared)
                tanh = jnp.tanh(inner)
                half = 0.5 + 0.5 * tanh
                out.ref[0, :, cols] = (pre * half).astype(BF16)
                slope = half + pre * (0.5 * (1.0 - tanh * tanh)) * (
                    0.7978845608028654 + 0.10703222440890037 * squared
                )
                grad = (nt(gfl[...], downs[at]()[cols, :]) * slope).astype(BF16)
                out.ref[1, :, cols] = grad
                vec_out.ref[pl.ds(block, 1), cols] = jnp.sum(grad.astype(F32), axis=0, keepdims=True)
            out.go()
        for start in range(0, depth, step):
            cols = slice(start, start + step)
            value = nt(acts[0].ref[1], ups[0]()[cols, :])
            for at in range(1, blocks):
                value = value + nt(acts[at].ref[1], ups[at]()[cols, :])
            back[:, cols] = value

        unit, inverse = normalize(x_ref[0:width].astype(F32) + branch_out.ref[...])
        vec_out.ref[5:6, :] = jnp.sum(back[...] * unit, axis=0, keepdims=True)
        vec_out.ref[6:7, :] = jnp.sum(back[...], axis=0, keepdims=True)
        mixed = norm_back(back[...], wide(scale2_ref), unit, inverse)
        mixed_out.ref[...] = mixed
        mixed_out.go()
        low = (gate_in()[:, 0:1] * wide(grad_in()) + mixed).astype(BF16)
        low_out.ref[...] = low
        low_out.go()
        vec_out.ref[7:8, :] = jnp.sum(low.astype(F32), axis=0, keepdims=True)
        value = nt(low, ow()[...]).astype(BF16)
        gout.ref[0:width] = value
        product = value.astype(F32) * wide(attended)
        high = product.astype(BF16)
        rest = (product - high.astype(F32)).astype(BF16)
        member = lax.broadcasted_iota(I32, (16, depth), 1) // HD
        ones = jnp.where(member == lax.broadcasted_iota(I32, (16, depth), 0), 1.0, 0.0).astype(BF16)
        delta = nt(ones, high) + nt(ones, rest)
        for head in range(H):
            for j in range(tiles):
                lot = (head // 2) * tiles + j
                at = (head % 2) * TILE
                delta_out.ref[lot : lot + 1, at : at + TILE] = delta[head : head + 1, j * TILE : (j + 1) * TILE]
        gout.ref[width:] = jnp.zeros_like(gout.ref[width:])
        for i, part in enumerate(three_parts(lse.ref[...])):
            gout.ref[width : width + lots, i * 2 * TILE : (i + 1) * 2 * TILE] = part
        for i, part in enumerate(three_parts(delta_out.ref[...])):
            gout.ref[width + extra : width + extra + lots, i * 2 * TILE : (i + 1) * 2 * TILE] = part
        gout.go()
        for start in range(0, depth, step):
            cols = slice(start, start + step)
            value = nn(acts[0].ref[0], downs[0]()[:, cols])
            for at in range(1, blocks):
                value = value + nn(acts[at].ref[0], downs[at]()[:, cols])
            feed_out.ref[:, cols] = value

    low = shape_of((width, depth), BF16)
    total = shape_of((width, depth), F32)
    stats = shape_of((lots, 2 * TILE), F32)
    return streamed(
        "far_and_feed", kernel, [spans, core],
        [query_bias, value_bias, scale, offset, out_bias, scale2, offset2, up_bias],
        [full(far)] + [columns(qkv_weight, i * depth, depth) for i in range(3)]
        + [full(a) for a in (routed, queries, acc, near_lse, gate, grad_routed, out_weight)]
        + [part(at) for at in range(blocks) for part in (up_part, down_part)],
        [low, low, low, shape_of((3, width, depth), BF16), stats, total, shape_of((2, 8, width), F32)]
        + [shape_of((2, width, depth), BF16)] * blocks
        + [total, shape_of((width + 2 * extra, depth), BF16), total, low, stats, shape_of((16, depth), F32)],
        scratch=[
            VMEM((width, width), F32), SMEM((2 * tiles,), I32), VMEM((width, depth), BF16),
            VMEM((width, depth), F32),
        ],
        scalar_outs=[shape_of((2 * tiles,), I32)],
        split=(3,),
    )


def feed_grads(got, bit, pack, far_pack, own):
    width, depth = pack.shape[1:]
    step = 256

    def kernel(scalars, small, fetches, sends, scratch, scalar_outs):
        second, own_grad, far_second, got_grad, gfl, far_gfl, own_hidden, got_hidden = fetches
        send, keep = sends
        bit = scalars[0][0]

        def up(ref):
            for at in range(0, depth, step):
                cols = slice(at, at + step)
                value = tn(second()[...], own_grad()[:, cols]) + tn(far_second()[...], got_grad()[:, cols])
                ref[:, cols] = value.astype(BF16)

        def down(ref):
            for at in range(0, depth, step):
                rows = slice(at, at + step)
                value = tn(own_hidden()[:, rows], gfl()[...]) + tn(got_hidden()[:, rows], far_gfl()[...])
                ref[rows, :] = value.astype(BF16)

        up(scratch[0].at[bit])
        down(scratch[0].at[1 - bit])
        for send_out, side in ((keep, 0), (send, 1)):
            send_out.copies = [pltpu.make_async_copy(scratch[0].at[side], send_out.target, send_out.sem.at[0])]
            send_out.go()

    half = shape_of((depth, depth), BF16)
    return streamed(
        "feed_grads", kernel, [jnp.reshape(bit, (1,)).astype(I32)], [],
        [row_of(pack, 0), row_of(own, 1), row_of(far_pack, 0), row_of(got, 1),
         row_of(pack, 1), row_of(far_pack, 1), row_of(own, 0), row_of(got, 0)],
        [half, half],
        scratch=[VMEM((2, depth, depth), BF16)],
    )


def own_back(part, parts, q, k, v, gout, lse, delta, fk, fv, lines, spans, far_spans):
    width, depth = q.shape
    tiles = width // TILE
    some = depth // parts
    pairs = some // PAIR
    base = part * pairs * tiles

    def kernel(scalars, small, fetches, sends, scratch, scalar_outs):
        q_in, k_in, v_in, g_in, fk_in, fv_in, lse_in, delta_in, lines_in = fetches
        dq, dk, dv = sends
        bias, far_bias, turned, far_turned, span, far_span, dq_turned = scratch
        lines_ref = lines_in()
        fill_bias(bias, lines_ref[0], lines_ref[0], -1.0)
        fill_bias(far_bias, lines_ref[1], lines_ref[0], -2.0)
        store_spans(span, scalars[0], scalars[0], tiles)
        store_spans(far_span, scalars[1], scalars[0], tiles)
        k_ref, fk_ref, q_ref, g_ref, v_ref, fv_ref = k_in(), fk_in(), q_in(), g_in(), v_in(), fv_in()
        lse_ref, delta_ref = lse_in(), delta_in()
        turned[...] = k_ref[...].T
        far_turned[...] = fk_ref[...].T
        dk.ref[...] = jnp.zeros_like(dk.ref)
        dv.ref[...] = jnp.zeros_like(dv.ref)

        def pieces(j, pair):
            cols = pl.ds(pl.multiple_of(pair * PAIR, PAIR), PAIR)
            rows = pl.ds(pl.multiple_of(j * TILE, TILE), TILE)
            query = stacked_heads(q_ref[rows, cols]) * SCALE
            grad = stacked_heads(g_ref[rows, cols])
            one = pl.ds(base + pair * tiles + j, 1)
            return cols, rows, query, grad, lse_ref[one], delta_ref[one]

        def local(n, j, pair):
            cols, rows, query, grad, top, delta = pieces(j, pair)
            near = pl.ds(pl.multiple_of(span[j] * TILE, TILE), n * TILE)
            weights = jnp.exp(nt(k_ref[near, cols], query) + twice(bias[near, rows]) - top)
            dscore = (weights * (nt(v_ref[near, cols], grad) - delta)).astype(BF16)
            dk.ref[near, cols] += nn(dscore, query)
            dv.ref[near, cols] += nn(weights.astype(BF16), grad)
            dq_turned[cols, rows] = own_blocks(nn(turned[cols, near], dscore))

        def remote(n, j, pair):
            cols, rows, query, grad, top, delta = pieces(j, pair)
            far = pl.ds(pl.multiple_of(far_span[j] * TILE, TILE), n * TILE)
            weights = jnp.exp(nt(fk_ref[far, cols], query) + twice(far_bias[far, rows]) - top)
            dscore = (weights * (nt(fv_ref[far, cols], grad) - delta)).astype(BF16)
            dq_turned[cols, rows] += own_blocks(nn(far_turned[cols, far], dscore))

        over_tiles(span, tiles, pairs, 1, local)
        over_tiles(far_span, tiles, pairs, 1, remote)
        dq.ref[...] = (dq_turned[...].T * SCALE).astype(BF16)

    total = shape_of((width, some), F32)
    return streamed(
        "own_back", kernel, [spans, far_spans], [],
        [columns(a, part * some, some) for a in (q, k, v)]
        + [(gout, lambda ref, scalars: ref.at[0:width, part * some : (part + 1) * some], (width, some))]
        + [columns(a, part * some, some) for a in (fk, fv)]
        + [full(lse), full(delta), full(lines)],
        [shape_of((width, some), BF16), total, total],
        scratch=[
            VMEM((width, width), F32), VMEM((width, width), F32),
            VMEM((some, width), BF16), VMEM((some, width), BF16),
            SMEM((2 * tiles,), I32), SMEM((2 * tiles,), I32), VMEM((some, width), F32),
        ],
    )


def other_back(fgout, core, spans, far_spans, fq, k, v, lines, grads, low, vec):
    width, depth = k.shape
    tiles = width // TILE
    parts = len(grads)
    some = depth // parts
    pairs = some // PAIR
    lots = depth // PAIR * tiles
    extra = -(-lots // 16) * 16
    half = depth // 2

    def kernel(scalars, small, fetches, sends, scratch, scalar_outs):
        g_in, fq_in, k_in, v_in, lines_in, low_in, vec_in = fetches[:7]
        pieces = fetches[7:]
        halves = sends[:4]
        dq, dk, dv, vec_out = sends[4:]
        bias, span, stat, dk_sum, dv_sum = scratch
        lines_ref = lines_in()
        fill_bias(bias, lines_ref[0], lines_ref[1], -1.0)
        store_spans(span, scalars[1], scalars[2], tiles)
        g_ref = g_in()
        for i in range(2):
            block = g_ref[width + i * extra : width + i * extra + lots]
            stat[i] = (
                block[:, 0 : 2 * TILE].astype(F32)
                + block[:, 2 * TILE : 4 * TILE].astype(F32)
                + block[:, 4 * TILE : 6 * TILE].astype(F32)
            )
        fq_ref, k_ref, v_ref = fq_in(), k_in(), v_in()
        for part in range(parts):
            place = slice(part * some, (part + 1) * some)
            dq.ref[:, place] = pieces[3 * part]()[...]
            dk_sum[:, place] = pieces[3 * part + 1]()[...]
            dv_sum[:, place] = pieces[3 * part + 2]()[...]

        def work(n, j, pair):
            cols = pl.ds(pl.multiple_of(pair * PAIR, PAIR), PAIR)
            rows = pl.ds(pl.multiple_of(j * TILE, TILE), TILE)
            one = pl.ds(pair * tiles + j, 1)
            query = stacked_heads(fq_ref[rows, cols]) * SCALE
            grad = stacked_heads(g_ref[rows, cols])
            near = pl.ds(pl.multiple_of(span[j] * TILE, TILE), n * TILE)
            scores = nt(k_ref[near, cols], query) + twice(bias[near, rows])
            weights = jnp.exp(scores - stat[0, one])
            dscore = (weights * (nt(v_ref[near, cols], grad) - stat[1, one])).astype(BF16)
            dk_sum[near, cols] += nn(dscore, query)
            dv_sum[near, cols] += nn(weights.astype(BF16), grad)

        over_tiles(span, tiles, depth // PAIR, 1, work)
        dk.ref[...] = dk_sum[...].astype(BF16)
        dv.ref[...] = dv_sum[...].astype(BF16)
        low_ref = low_in()
        cols = pl.ds(pl.multiple_of((1 - scalars[0][0]) * half, TILE), half)
        for out, ref in zip(halves, (dq.ref, dk.ref, dv.ref, low_ref)):
            out.ref[...] = ref[:, cols]
            out.go()
        vec_out.ref[...] = vec_in()[...]
        vec_out.ref[8:9, :] = jnp.sum(wide(dq.ref), axis=0, keepdims=True)
        vec_out.ref[9:10, :] = jnp.sum(wide(dv.ref), axis=0, keepdims=True)

    flat = [piece for grad in grads for piece in grad]
    low_shape = shape_of((width, depth), BF16)
    return streamed(
        "other_back", kernel, [core, spans, far_spans], [],
        [full(a) for a in (fgout, fq, k, v, lines, low, vec)] + [full(a) for a in flat],
        [shape_of((width, half), BF16)] * 4 + [low_shape] * 3 + [shape_of((16, depth), F32)],
        scratch=[
            VMEM((width, width), F32), SMEM((2 * tiles,), I32), VMEM((2, lots, 2 * TILE), F32),
            VMEM((width, depth), F32), VMEM((width, depth), F32),
        ],
    )


def last_grads(core, bit, normed, far_normed, pack, far_pack, dq, dk, dv, low, got):
    width, depth = dq.shape
    half = depth // 2

    def kernel(scalars, small, fetches, sends, scratch, scalar_outs):
        left, far_left, att, far_att, dq_in, dk_in, dv_in, low_in = fetches[:8]
        gots = fetches[8:]
        send, keep = sends
        turned = scratch[0]
        cols = pl.ds(pl.multiple_of(scalars[0][0] * half, TILE), half)
        for i, ref in enumerate((left, far_left, att, far_att)):
            turned[i // 2, :, (i % 2) * width : (i % 2 + 1) * width] = ref()[...].T
        for out, which in ((send, 1 - scalars[1][0]), (keep, scalars[1][0])):
            rows = pl.ds(pl.multiple_of(which * half, TILE), half)
            for i, part in enumerate((dq_in, dk_in, dv_in, low_in)):
                place = slice(i * half, (i + 1) * half)
                side = 0 if i < 3 else 1
                value = nn(turned[side, rows, 0:width], part()[:, cols])
                value = value + nn(turned[side, rows, width : 2 * width], gots[i]()[...])
                out.ref[:, place] = value.astype(BF16)
            out.go()

    shape = shape_of((half, 2 * depth), BF16)
    return streamed(
        "last_grads", kernel, [core, jnp.reshape(bit, (1,)).astype(I32)], [],
        [full(normed), full(far_normed), row_of(pack, 2), row_of(far_pack, 2)]
        + [full(a) for a in (dq, dk, dv, low) + tuple(got)],
        [shape, shape],
        scratch=[VMEM((2, depth, 2 * width), BF16)],
    )


def scatter(hot_ref, rows, slots_ref):
    hot = hot_ref[...]
    taken = jnp.max(hot.astype(F32), axis=-1, keepdims=True) > 0.0
    return jnp.where(taken, nn(hot, rows).astype(BF16), slots_ref[...])


def token_out(hot, tokens, routed, gate, branch, feed, down_bias, grad_routed, router, mixed, vec):
    slots, depth = tokens.shape
    width = branch.shape[0]

    def kernel(scalars, small, fetches, sends, scratch, scalar_outs):
        branch_in, feed_in, x_in, gate_in, grad_in, mixed_in, vec_in, hot_in, tok_in = fetches
        out, base, vec_out = sends
        total = branch_in()[...] + feed_in()[...] + wide(small[0])
        x = wide(x_in())
        gate = gate_in()[:, 0:1]
        grad = wide(grad_in())
        logit = jnp.sum(grad * total, axis=-1, keepdims=True) * gate * (1.0 - gate)
        base.ref[...] = grad + mixed_in()[...] + logit * wide(small[1])
        base.go()
        vec_out.ref[...] = vec_in()[...]
        vec_out.ref[12:13, :] = jnp.sum(x * logit, axis=0, keepdims=True)
        out.ref[...] = scatter(hot_in(), (x + gate * total).astype(BF16), tok_in())

    return streamed(
        "token_out", kernel, [], [down_bias, router],
        [full(branch), full(feed), head_rows(routed, width)]
        + [full(a) for a in (gate, grad_routed, mixed, vec, hot, tokens)],
        [shape_of((slots, depth), BF16), shape_of((width, depth), F32), shape_of((16, depth), F32)],
    )


def token_grad(dq, dk, dv, hot, cotangent, routed, base, scale, qkv_weight, vec):
    slots, depth = cotangent.shape
    width = base.shape[0]

    def kernel(scalars, small, fetches, sends, scratch, scalar_outs):
        dq_in, weight_q, dk_in, weight_k, dv_in, weight_v, x_in, base_in, vec_in, hot_in, cot_in = fetches
        out, vec_out = sends
        back = nt(dq_in()[...], weight_q()[...]) + nt(dk_in()[...], weight_k()[...])
        back = back + nt(dv_in()[...], weight_v()[...])
        unit, inverse = normalize(wide(x_in()))
        vec_out.ref[...] = vec_in()[...]
        vec_out.ref[10:11, :] = jnp.sum(back * unit, axis=0, keepdims=True)
        vec_out.ref[11:12, :] = jnp.sum(back, axis=0, keepdims=True)
        vec_out.go()
        rows = (base_in()[...] + norm_back(back, wide(small[0]), unit, inverse)).astype(BF16)
        out.ref[...] = scatter(hot_in(), rows, cot_in())

    return streamed(
        "token_grad", kernel, [], [scale],
        [
            full(dq), columns(qkv_weight, 0, depth), full(dk), columns(qkv_weight, depth, depth),
            full(dv), columns(qkv_weight, 2 * depth, depth), head_rows(routed, width),
            full(base), full(vec), full(hot), full(cotangent),
        ],
        [shape_of((slots, depth), BF16), shape_of((16, depth), F32)],
    )


AXES = ("rows", "seq")
SHIFT = {"c": 0, "x": 1, "z1": 2, "z2": 3}
BLOCK = 16
XY_FIRST = (("x", "y"), ("y", "x"), ("z1", "z1"), ("z2", "z2"))
YX_FIRST = (("y", "x"), ("x", "y"), ("z1", "z1"), ("z2", "z2"))


def swap(block, axes):
    route = []
    for row in range(lax.axis_size("rows")):
        axis = axes[row & 1]
        for seq in range(2):
            if axis == "y":
                other = row * 2 + (seq ^ 1)
            else:
                other = (row ^ (1 << SHIFT[axis])) * 2 + seq
            route.append((row * 2 + seq, other))
    return lax.ppermute(block, AXES, route)


def own_bit(axis):
    if axis == "y":
        return lax.axis_index("seq")
    return (lax.axis_index("rows") >> SHIFT[axis]) & 1


def stage_bit(axes, core):
    if axes[0] == axes[1]:
        return own_bit(axes[0])
    return jnp.where(core == 0, own_bit(axes[0]), own_bit(axes[1]))


def half_of(block, which):
    half = block.shape[0] // 2
    return lax.dynamic_slice_in_dim(block, which * half, half, 0)


def add_low(left, right):
    return (left.astype(F32) + right.astype(F32)).astype(BF16)


def after(value, *others):
    return lax.optimization_barrier((value, *others))[0]


def over_blocks(total):
    extra = BLOCK
    size = lax.axis_size("rows")
    while extra < size:
        route = [(i * 2 + j, (i ^ extra) * 2 + j) for i in range(size) for j in range(2)]
        got = lax.ppermute(total, AXES, route)
        total = (total.astype(F32) + got.astype(F32)).astype(total.dtype)
        extra *= 2
    return total


class Order:
    def __init__(self):
        self.tail = None

    def run(self, call, lead, *args):
        if self.tail is not None:
            leaves, tree = jax.tree.flatten(lead)
            leaves = lax.optimization_barrier(tuple(leaves) + (self.tail,))[:-1]
            lead = jax.tree.unflatten(tree, leaves)
        result = call(lead, *args)
        self.tail = jax.tree.leaves(result)[-1]
        return result


def two_parts(block):
    high = block.astype(BF16)
    return jnp.concatenate([high, (block - high.astype(F32)).astype(BF16)], axis=1)


def from_parts(block):
    half = block.shape[1] // 2
    return block[:, :half].astype(F32) + block[:, half:].astype(F32)


class Sum:
    def __init__(self, order, send, keep, stages):
        self.order, self.keep, self.stages, self.at = order, keep, stages, 1
        self.small, self.riding = None, False
        self.got = swap(send, stages[0])

    @classmethod
    def joined(cls, order, parts):
        new = cls.__new__(cls)
        new.order, new.stages, new.at = order, parts[0].stages, parts[0].at
        new.small, new.riding = None, False
        new.keep = tuple(part.keep for part in parts)
        new.got = tuple(part.got for part in parts)
        return new

    def take(self):
        if not self.riding:
            return self.got
        rows = self.got.shape[0] - self.small.shape[0]
        self.small = self.small + from_parts(self.got[rows:])
        self.riding = False
        return self.got[:rows]

    def post(self, send, axes, ride):
        if ride and self.small is not None:
            send = jnp.concatenate([send, two_parts(self.small)], axis=0)
            self.riding = True
        return swap(send, axes)

    def reduce(self):
        if self.at == len(self.stages):
            self.keep = over_blocks(self.order.run(add_low, self.take(), self.keep))
            self.got = swap(self.keep, self.stages[-1])
            return
        axes = self.stages[self.at]
        bit = stage_bit(axes, own_bit("c"))

        def add(got, keep, which):
            if isinstance(got, tuple):
                return jnp.concatenate([add(g, k, which) for g, k in zip(got, keep)], axis=1)
            return add_low(half_of(keep, which), half_of(got, which))

        arrived = self.take()
        send = self.order.run(lambda got, keep: add(got, keep, 1 - bit), arrived, self.keep)
        got = self.post(send, axes, True)
        self.keep = self.order.run(lambda got, keep: add(got, keep, bit), arrived, self.keep)
        self.got = got
        self.at += 1

    def gather(self):
        self.at -= 1
        self.keep = self.order.run(lambda got, keep: jnp.concatenate([keep, got]), self.got, self.keep)
        self.got = self.post(self.keep, self.stages[self.at - 1], self.at == 1)
        if self.at == 1:
            self.blocks = [(self.keep, 0, 0), (swap(self.keep, ("c", "c")), 1, 0)]

    def rest(self):
        self.got = self.order.run(lambda got: got, self.got)
        self.blocks += [(self.got, 0, 1), (swap(self.got, ("c", "c")), 1, 1)]
        self.take()


def shard_of(stages, core):
    index = jnp.int32(0)
    for axes in stages:
        index = index * 2 + stage_bit(axes, core)
    return index


SHARDS = 8


def place_kernel(kind, rows, count, info_ref, *rest):
    blocks = rest[:count]
    first_ref, second_ref, low, full, sems = rest[-5:]
    depth = blocks[0].shape[1]
    lots = [info_ref[3 * i + 2] for i in range(count)]
    tops = [info_ref[3 * i + 1] for i in range(count)]

    def pull(i, s):
        src = pl.ds(pl.multiple_of((s ^ info_ref[3 * i]) * rows, rows), rows)
        return pltpu.make_async_copy(blocks[i].at[src], low.at[i, pl.ds(s * rows, rows)], sems.at[0, i, s])

    def push(i, s, top):
        src = full.at[i, pl.ds(s * rows, rows)]
        lot = lots[i]
        if kind == "feed":
            copies = []
            size = depth // 2
            for t in range(2):
                at = (lot + 2 * t) * size
                if top == 0:
                    to = first_ref.at[pl.ds(s * rows, rows), pl.ds(pl.multiple_of(at, 128), size)]
                else:
                    to = second_ref.at[pl.ds(pl.multiple_of(at + s * rows, rows), rows)]
                copies.append(pltpu.make_async_copy(src.at[:, pl.ds(t * size, size)], to, sems.at[1 + t, i, s]))
            return copies
        part = depth // 4
        row = pl.ds(pl.multiple_of((tops[i] * SHARDS + s) * rows, rows), rows)
        copies = []
        for t in range(4):
            target = first_ref if t < 3 else second_ref
            at = (2 * t + lot) * part if t < 3 else lot * part
            copies.append(
                pltpu.make_async_copy(
                    src.at[:, pl.ds(t * part, part)],
                    target.at[row, pl.ds(pl.multiple_of(at, 128), part)],
                    sems.at[1 + t, i, s],
                )
            )
        return copies

    def start(i, s):
        if kind != "feed":
            for copy in push(i, s, 0):
                copy.start()
            return
        for top in range(2):

            @pl.when(tops[i] == top)
            def _(top=top):
                for copy in push(i, s, top):
                    copy.start()

    for i in range(count):
        for s in range(SHARDS):
            pull(i, s).start()
    for i in range(count):
        for s in range(SHARDS):
            pull(i, s).wait()
            dst = slice(s * rows, (s + 1) * rows)
            full[i, dst] = low[i, dst].astype(F32)
            start(i, s)
    for i in range(count):
        for s in range(SHARDS):
            for copy in push(i, s, 0):
                copy.wait()


def place(kind, rows, blocks, info, targets, shapes):
    hbm = pl.BlockSpec(memory_space=pltpu.HBM)
    targets = targets or ()
    count = len(blocks)
    return pl.pallas_call(
        functools.partial(place_kernel, kind, rows, count),
        out_shape=tuple(jax.ShapeDtypeStruct(s, F32) for s in shapes),
        in_specs=[pl.BlockSpec(memory_space=pltpu.SMEM)] + [hbm] * (count + len(targets)),
        out_specs=(hbm, hbm),
        scratch_shapes=[
            VMEM((count, rows * SHARDS, blocks[0].shape[1]), BF16),
            VMEM((count, rows * SHARDS, blocks[0].shape[1]), F32),
            pltpu.SemaphoreType.DMA((5, count, SHARDS)),
        ],
        input_output_aliases={1 + count: 0, 2 + count: 1} if targets else {},
        compiler_params=pltpu.CompilerParams(vmem_limit_bytes=62 << 20),
        cost_estimate=pl.CostEstimate(flops=int(LENGTH["place"] * RATE), bytes_accessed=0, transcendentals=0),
        name="place",
    )(info, *blocks, *targets)


def body(
    tokens,
    cotangent,
    segment_ids,
    routing,
    qkv_weight,
    query_bias,
    value_bias,
    out_weight,
    out_bias,
    first_scale,
    first_offset,
    second_scale,
    second_offset,
    up_weight,
    up_bias,
    down_weight,
    down_bias,
    router_weight,
):
    row_count, slots, depth = tokens.shape
    hidden = up_weight.shape[1]
    count = slots // 2
    width = -(-count // 128) * 128
    core = own_bit("c")
    seat = jnp.reshape(core, (1,)).astype(jnp.int32)
    pos = jnp.reshape(lax.axis_index("seq"), (1,)).astype(jnp.int32)
    tokens = tokens.reshape(slots, depth)
    cotangent = cotangent.reshape(slots, depth)
    routes = routing.reshape(2, 1, slots)
    segs = segment_ids.reshape(2, 1, slots)
    qb, vb, ob, s1, o1, s2, o2, db, rw = (
        v.reshape(1, depth)
        for v in (query_bias, value_bias, out_bias, first_scale, first_offset, second_scale,
                  second_offset, down_bias, router_weight)
    )
    ub = up_bias.reshape(1, hidden)

    order = Order()
    routed, grad_routed, hot, spans = pick_rows(pos, routes, segs, tokens, cotangent, count, width)
    far = swap(routed, ("y", "y"))
    q, k, v, normed, gate, acc, near_lse = near_attention(spans, routed, qkv_weight, qb, vb, s1, o1, rw)
    far_normed = swap(normed, ("c", "c"))
    fq, fk, fv, pack, lse, branch, lines, *rest, far_spans = order.run(
        far_and_feed, far, spans, seat, routed, qkv_weight, qb, vb, s1, o1, count, q, acc, near_lse,
        out_weight, ob, s2, o2, gate, grad_routed, up_weight, ub, down_weight
    )
    *acts, feed_sum, gout, mixed, low, delta, vec = rest
    fgout = swap(gout, ("y", "y"))
    far_pack = swap(pack, ("c", "c"))
    sends = [swap(send, ("c", "c")) for send in acts[0::2]]

    plans = (XY_FIRST, XY_FIRST, YX_FIRST)
    first_bits = [stage_bit(plan[0], core) for plan in plans]

    def feed_sums(pair):
        send, keep = order.run(feed_grads, sends[pair], first_bits[pair], pack, far_pack, acts[2 * pair + 1])
        return Sum(order, send, keep, plans[pair])

    def own_part(part):
        return order.run(
            lambda q: own_back(part, 2, q, k, v, gout, lse, delta, fk, fv, lines, spans, far_spans), q
        )

    grads = [own_part(0)]
    one = feed_sums(0)
    fgout = order.run(lambda got: got, fgout)
    two = feed_sums(1)
    grads.append(own_part(1))
    one.got = order.run(lambda got: got, one.got)
    *last_sends, dq, dk, dv, vec = order.run(
        other_back, fgout, seat, spans, far_spans, fq, k, v, lines, grads, low, vec
    )
    gots = [swap(send, ("c", "c")) for send in last_sends]
    both = Sum.joined(order, (one, two))
    both.reduce()
    send, keep = order.run(
        lambda got, *rest: last_grads(
            seat, first_bits[2], normed, far_normed, pack, far_pack, dq, dk, dv, low, (got,) + rest
        ), *gots
    )
    three = Sum(order, send, keep, plans[2])
    both.reduce()
    out_tokens, base, vec = order.run(
        token_out, hot, tokens, routed, gate, branch, feed_sum, db, grad_routed, rw, mixed, vec
    )
    grad_tokens, vec = order.run(token_grad, dq, dk, dv, hot, cotangent, routed, base, s1, qkv_weight, vec)
    three.small = vec

    kinds = {
        "feed": ((depth, hidden), (hidden, depth)),
        "last": ((depth, 3 * depth), (depth, depth)),
    }
    targets = {"feed": None, "last": None}
    rows = {"feed": depth // 8, "last": depth // 16}

    def put(kind, some):
        blocks, info = [], []
        for block, other, half in some:
            owner = core if other == 0 else 1 - core
            own = shard_of(plans[0] if kind == "feed" else plans[2], owner)
            blocks.append(block)
            info += [own % 8, own // 8 ^ half, owner]
        info = jnp.stack(info).astype(jnp.int32)
        targets[kind] = order.run(
            lambda block, *rest: place(kind, rows[kind], rest + (block,), info, targets[kind], kinds[kind]),
            blocks[-1], *blocks[:-1]
        )

    both.reduce()
    three.reduce()
    both.reduce()
    both.gather()
    both.gather()
    three.reduce()
    three.reduce()
    both.gather()
    three.reduce()
    three.gather()
    three.gather()
    put("feed", both.blocks[:2])
    both.rest()
    three.gather()
    put("last", three.blocks)
    put("feed", both.blocks[2:])
    three.rest()
    vec = three.small + swap(three.small, ("c", "c"))
    put("last", three.blocks[2:3])
    put("last", three.blocks[3:])
    vec = over_blocks(vec)
    grad_up, grad_down = targets["feed"]
    grad_qkv, grad_out = targets["last"]
    return (
        out_tokens.reshape(row_count, slots, depth),
        grad_tokens.reshape(row_count, slots, depth),
        grad_qkv,
        vec[8],
        vec[9],
        grad_out,
        vec[7],
        vec[10],
        vec[11],
        vec[5],
        vec[6],
        grad_up,
        vec[0:4].reshape(hidden),
        grad_down,
        vec[4],
        vec[12],
    )


def solution(mesh):
    split = P("rows", "seq", None)
    return jax.shard_map(
        body,
        mesh=mesh,
        in_specs=(split, split, P("rows", None), P("rows", None)) + (P(),) * 14,
        out_specs=(split, split) + (P(),) * 14,
        check_vma=False,
    )
```

```python
import functools

import jax
import jax.numpy as jnp
from jax import lax
from jax.experimental import pallas as pl
from jax.experimental.pallas import tpu as pltpu
from jax.sharding import PartitionSpec as P

H = 12
HD = 64
PAIR = 2 * HD
TILE = 128
NEG = -1e30
SCALE = HD ** (-0.5)
RATE = 1.15e9
LENGTH = {
    "pick_rows": 6.0,
    "near_attention": 14.0,
    "far_and_feed": 36.0,
    "feed_grads": 0.1,
    "own_back": 0.1,
    "other_back": 1.0,
    "token_out": 0.1,
    "last_grads": 0.1,
    "token_grad": 14.0,
    "place": 1.0,
}
F32 = jnp.float32
BF16 = jnp.bfloat16
I32 = jnp.int32
VMEM = pltpu.VMEM
SMEM = pltpu.SMEM


def nn(a, b):
    return lax.dot_general(a, b, (((1,), (0,)), ((), ())), preferred_element_type=F32)


def nt(a, b):
    return lax.dot_general(a, b, (((1,), (1,)), ((), ())), preferred_element_type=F32)


def tn(a, b):
    return lax.dot_general(a, b, (((0,), (0,)), ((), ())), preferred_element_type=F32)


def shape_of(shape, kind):
    return jax.ShapeDtypeStruct(shape, kind)


class Fetch:
    def __init__(self, copies, target):
        self.copies, self.target = copies, target
        self.waiting = set(range(len(copies)))
        for copy in copies:
            copy.start()

    def __call__(self, piece=None):
        for i in sorted(self.waiting) if piece is None else [piece]:
            if i in self.waiting:
                self.copies[i].wait()
                self.waiting.discard(i)
        return self.target


class Send:
    def __init__(self, buffer, target, sems, pieces):
        self.ref, self.target, self.sem, self.copies = buffer, target, sems, []
        for i in range(pieces):
            source, to = (buffer, target) if pieces == 1 else (buffer.at[i], target.at[i])
            self.copies.append(pltpu.make_async_copy(source, to, sems.at[i]))
        self.left = set(range(pieces))

    def go(self, piece=None):
        for i in sorted(self.left) if piece is None else [piece]:
            if i in self.left:
                self.copies[i].start()
                self.left.discard(i)

    def wait(self):
        self.go()
        for copy in self.copies:
            copy.wait()


def streamed(name, kernel, scalars, small, large, outs, scratch=(), scalar_outs=(), room=62, split=()):
    arrays, plans = [], []
    for array, parts, extent in large:
        at = next((i for i, a in enumerate(arrays) if a is array), None)
        if at is None:
            at = len(arrays)
            arrays.append(array)
        if parts is None or callable(parts):
            parts = [(parts, None)]
        plans.append((at, parts, extent))
    most_in = max(len(p) for _, p, _ in plans)
    counts = [o.shape[0] if i in split else 1 for i, o in enumerate(outs)]

    def wrapped(*refs):
        refs = list(refs)

        def take(count):
            head = refs[:count]
            del refs[:count]
            return head

        scalar_refs = take(len(scalars))
        small_refs = take(len(small))
        array_refs = take(len(arrays))
        out_refs = take(len(outs))
        scalar_out_refs = take(len(scalar_outs))
        landing = take(len(plans))
        staging = take(len(outs))
        in_sems, out_sems = take(2)
        fetches = []
        for i, (at, parts, _) in enumerate(plans):
            copies = []
            for j, (source, place) in enumerate(parts):
                start = array_refs[at] if source is None else source(array_refs[at], scalar_refs)
                to = landing[i] if place is None else place(landing[i])
                copies.append(pltpu.make_async_copy(start, to, in_sems.at[i, j]))
            fetches.append(Fetch(copies, landing[i]))
        sends = [Send(staging[i], out_refs[i], out_sems.at[i], counts[i]) for i in range(len(outs))]
        kernel(scalar_refs, small_refs, fetches, sends, refs, scalar_out_refs)
        for fetch in fetches:
            fetch()
        for send in sends:
            send.go()
        for send in sends:
            send.wait()

    hbm = pl.BlockSpec(memory_space=pltpu.HBM)
    return pl.pallas_call(
        wrapped,
        out_shape=tuple(outs) + tuple(scalar_outs),
        in_specs=[pl.BlockSpec(memory_space=SMEM)] * len(scalars)
        + [pl.BlockSpec(memory_space=VMEM)] * len(small)
        + [hbm] * len(arrays),
        out_specs=tuple([hbm] * len(outs) + [pl.BlockSpec(memory_space=SMEM)] * len(scalar_outs)),
        scratch_shapes=[VMEM(extent, arrays[at].dtype) for at, _, extent in plans]
        + [VMEM(o.shape, o.dtype) for o in outs]
        + [pltpu.SemaphoreType.DMA((len(plans), most_in)), pltpu.SemaphoreType.DMA((len(outs), max(counts)))]
        + list(scratch),
        compiler_params=pltpu.CompilerParams(vmem_limit_bytes=room << 20),
        cost_estimate=pl.CostEstimate(flops=int(LENGTH[name] * RATE), bytes_accessed=0, transcendentals=0),
        name=name,
    )(*scalars, *small, *arrays)


def full(array):
    return (array, None, array.shape)


def row_of(array, index):
    return (array, lambda ref, scalars: ref.at[index], array.shape[1:])


def head_rows(array, count):
    return (array, lambda ref, scalars: ref.at[0:count], (count,) + array.shape[1:])


def columns(array, start, count):
    return (array, lambda ref, scalars: ref.at[:, start : start + count], (array.shape[0], count))


def wide(ref):
    return ref[...].astype(F32)


def normalize(values):
    center = values - jnp.mean(values, axis=-1, keepdims=True)
    inverse = lax.rsqrt(jnp.mean(center * center, axis=-1, keepdims=True) + 1e-06)
    return center * inverse, inverse


def norm_back(grad, scale, unit, inverse):
    scaled = grad * scale
    first = jnp.mean(scaled, axis=-1, keepdims=True)
    second = jnp.mean(scaled * unit, axis=-1, keepdims=True)
    return inverse * (scaled - first - unit * second)


def tile_spans(line, count, out_ref):
    width = line.shape[1]
    lane = lax.broadcasted_iota(I32, (1, width), 1)
    tiles = width // TILE
    for i in range(tiles):
        inside = (lane >= i * TILE) & (lane < min((i + 1) * TILE, count))
        out_ref[i] = jnp.min(jnp.where(inside, line, 1e9)).astype(I32)
        out_ref[tiles + i] = jnp.max(jnp.where(inside, line, -1e9)).astype(I32)


def pick_rows(pos, routes, segs, tokens, cotangent, count, width):
    slots, depth = tokens.shape

    def kernel(scalars, small, fetches, sends, scratch, scalar_outs):
        tok, cot = fetches
        routed, grad, hot_out = sends
        own_first = scalars[0][0] == 0

        def half(ref, size):
            both = ref[...]
            return jnp.where(own_first, both[:, 0:size], both[:, slots : slots + size])

        lane = lax.broadcasted_iota(I32, (slots, width), 1)
        slot = lax.broadcasted_iota(I32, (slots, width), 0)
        chosen = (slot == half(small[0], width)) & (lane < count)
        taken = jnp.max(jnp.where(chosen, 1.0, 0.0), axis=-1, keepdims=True)
        before = lax.broadcasted_iota(I32, (slots, slots), 0) < lax.broadcasted_iota(I32, (slots, slots), 1)
        before = jnp.where(before, 1.0, 0.0).astype(BF16)
        rank = tn(before, jnp.broadcast_to(taken, (slots, TILE)).astype(BF16))[:, 0:1]
        rank = jnp.where(taken > 0.0, rank, -1.0)
        hot = jnp.where(lane.astype(F32) == rank, 1.0, 0.0).astype(BF16)
        hot_out.ref[...] = hot
        hot_out.go()
        groups = jnp.broadcast_to(half(small[1], slots).astype(F32), (8, slots)).astype(BF16)
        line = nn(groups, hot)
        line = jnp.where(lax.broadcasted_iota(I32, (8, width), 1) < count, line, -1.0)
        routed.ref[0:width] = tn(hot, tok()[...]).astype(BF16)
        routed.ref[width:] = jnp.zeros_like(routed.ref[width:])
        routed.ref[width : width + 8, 0:width] = line.astype(BF16)
        routed.go()
        grad.ref[...] = tn(hot, cot()[...]).astype(BF16)
        tile_spans(line[0:1], count, scalar_outs[0])

    return streamed(
        "pick_rows", kernel, [pos], [routes, segs],
        [full(tokens), full(cotangent)],
        [shape_of((width + 16, depth), BF16), shape_of((width, depth), BF16), shape_of((slots, width), BF16)],
        scalar_outs=[shape_of((2 * (width // TILE),), I32)],
    )


def key_span(keys, queries, j, tiles):
    low, high = queries[j], queries[tiles + j]
    first, last = jnp.int32(tiles), jnp.int32(-1)
    for t in range(tiles):
        meets = (keys[tiles + t] >= low) & (keys[t] <= high)
        first = jnp.where(meets & (first == tiles), t, first)
        last = jnp.where(meets, t, last)
    return jnp.minimum(first, tiles - 1), jnp.maximum(last - first + 1, 0)


def store_spans(ref, keys, queries, tiles):
    for j in range(tiles):
        first, many = key_span(keys, queries, j, tiles)
        ref[j] = first
        ref[tiles + j] = many


def fill_bias(bias_ref, key_line, query_line, key_pad):
    keys = jnp.where(key_line < 0.0, key_pad, key_line).T[:, 0:1]
    bias_ref[...] = jnp.where(keys == query_line[0:1], 0.0, NEG)


def fill_row_bias(bias_ref, key_line, query_line, key_pad):
    keys = jnp.where(key_line < 0.0, key_pad, key_line)[0:1]
    bias_ref[...] = jnp.where(query_line.T[:, 0:1] == keys, 0.0, NEG)


def first_head():
    return lax.broadcasted_iota(I32, (1, PAIR), 1) < HD


def attend_rows(query, keys, values, bias):
    first = first_head()
    zero = jnp.zeros_like(query)
    wide_values = jnp.concatenate([values, jnp.ones_like(values)], axis=1)
    sums, tops = [], []
    for head in range(2):
        some = jnp.where(first if head == 0 else jnp.logical_not(first), query, zero) * SCALE
        scores = nt(some, keys) + bias
        top = jnp.max(scores, axis=1, keepdims=True)
        sums.append(nn(jnp.exp(scores - top).astype(BF16), wide_values))
        tops.append(top)
    value = jnp.where(first, sums[0][:, 0:PAIR], sums[1][:, 0:PAIR])
    total = jnp.where(first, sums[0][:, PAIR:], sums[1][:, PAIR:])
    return value, total, jnp.where(first, tops[0], tops[1])


def stacked_heads(block):
    lane = lax.broadcasted_iota(I32, (1, PAIR), 1)
    zero = jnp.zeros_like(block)
    return jnp.concatenate([jnp.where(lane < HD, block, zero), jnp.where(lane >= HD, block, zero)], axis=0)


def own_blocks(block):
    return jnp.concatenate([block[0:HD, 0:TILE], block[HD:PAIR, TILE : 2 * TILE]], axis=0)


def twice(block):
    return jnp.concatenate([block, block], axis=1)


def over_tiles(span, tiles, pairs, lowest, work, group=3):
    def tile_step(j, carry):
        for n in range(lowest, tiles + 1):

            def branch(n=n):
                def group_step(i, inner):
                    for p in range(group):
                        work(n, j, i * group + p)
                    return inner

                lax.fori_loop(0, pairs // group, group_step, 0)

            pl.when(span[tiles + j] == n)(branch)
        return carry

    lax.fori_loop(0, tiles, tile_step, 0)


def project(normed, weights, qb, vb, q_ref, k_ref, v_ref, sends):
    depth = normed.shape[1]
    step = 256
    for part, (ref, weight) in enumerate(zip((k_ref, q_ref, v_ref), (weights[1], weights[0], weights[2]))):
        weight_ref = weight()
        for at in range(0, depth, step):
            value = nn(normed, weight_ref[:, at : at + step])
            if part == 1:
                value = value + qb[:, at : at + step]
            elif part == 2:
                value = value + vb[:, at : at + step]
            ref[:, at : at + step] = value.astype(BF16)
        sends[part].go()


def near_attention(spans, routed, qkv_weight, query_bias, value_bias, scale, offset, router):
    depth = routed.shape[1]
    width = routed.shape[0] - 16
    tiles = width // TILE
    pairs = depth // PAIR

    def kernel(scalars, small, fetches, sends, scratch, scalar_outs):
        qb, vb, scale_ref, offset_ref, router_ref = small
        q, k, v, normed, gate, acc, lse = sends
        bias, span = scratch
        x_ref = fetches[0]()
        x = x_ref[0:width].astype(F32)
        unit, _ = normalize(x)
        low = (unit * wide(scale_ref) + wide(offset_ref)).astype(BF16)
        normed.ref[...] = low
        normed.go()
        project(low, fetches[1:4], wide(qb), wide(vb), q.ref, k.ref, v.ref, (k, q, v))
        logit = jnp.sum(x * wide(router_ref), axis=-1, keepdims=True)
        gate.ref[...] = jnp.broadcast_to(1.0 / (1.0 + jnp.exp(-logit)), gate.ref.shape)
        gate.go()
        line = x_ref[width : width + 8, 0:width].astype(F32)
        fill_row_bias(bias, line, line, -1.0)
        store_spans(span, scalars[0], scalars[0], tiles)

        def work(n, j, pair):
            cols = pl.ds(pl.multiple_of(pair * PAIR, PAIR), PAIR)
            rows = pl.ds(pl.multiple_of(j * TILE, TILE), TILE)
            some = pl.ds(pl.multiple_of(span[j] * TILE, TILE), n * TILE)
            value, total, top = attend_rows(q.ref[rows, cols], k.ref[some, cols], v.ref[some, cols], bias[rows, some])
            acc.ref[rows, cols] = value / total
            lse.ref[rows, cols] = top + jnp.log(total)

        over_tiles(span, tiles, pairs, 1, work)

    low = shape_of((width, depth), BF16)
    total = shape_of((width, depth), F32)
    return streamed(
        "near_attention", kernel, [spans], [query_bias, value_bias, scale, offset, router],
        [full(routed)] + [columns(qkv_weight, i * depth, depth) for i in range(3)],
        [low, low, low, low, shape_of((width, TILE), F32), total, total],
        scratch=[VMEM((width, width), F32), SMEM((2 * tiles,), I32)],
    )


def three_parts(value):
    high = value.astype(BF16)
    rest = value - high.astype(F32)
    middle_part = rest.astype(BF16)
    return high, middle_part, (rest - middle_part.astype(F32)).astype(BF16)


def far_and_feed(far, spans, core, routed, qkv_weight, query_bias, value_bias, scale, offset, count,
                 queries, acc, near_lse, out_weight, out_bias, scale2, offset2, gate, grad_routed,
                 up_weight, up_bias, down_weight):
    depth = routed.shape[1]
    width = routed.shape[0] - 16
    tiles = width // TILE
    pairs = depth // PAIR
    lots = pairs * tiles
    extra = -(-lots // 16) * 16
    step = 256
    steps = depth // step
    blocks = up_weight.shape[1] // depth

    def block_of(at, scalars):
        own = scalars[1][0]
        return at // 2 * 2 + (1 - own if at % 2 == 0 else own)

    def up_part(at):
        def piece(i):
            def source(ref, scalars):
                start = pl.multiple_of(block_of(at, scalars) * depth + i * step, step)
                return ref.at[:, pl.ds(start, step)]
            return source, lambda ref: ref.at[:, i * step : (i + 1) * step]
        return (up_weight, [piece(i) for i in range(steps)], (depth, depth))

    def down_part(at):
        def part(ref, scalars):
            return ref.at[pl.ds(pl.multiple_of(block_of(at, scalars) * depth, step), depth)]
        return (down_weight, part, (depth, depth))

    def kernel(scalars, small, fetches, sends, scratch, scalar_outs):
        qb, vb, scale_ref, offset_ref, ob, scale2_ref, offset2_ref, ub = small
        far_in, weight_q, weight_k, weight_v, x_in, q_in, acc_in, lse_in, gate_in, grad_in, ow = fetches[:11]
        ups, downs = fetches[11::2], fetches[12::2]
        fq, fk, fv, pack, lse, branch_out, lines = sends[:7]
        acts = sends[7 : 7 + blocks]
        feed_out, gout, mixed_out, low_out, delta_out, vec_out = sends[7 + blocks :]
        bias, span, attended, back = scratch
        far_ref = far_in()
        far_line = far_ref[width : width + 8, 0:width].astype(F32)
        tile_spans(far_line[0:1], count, scalar_outs[0])
        unit, _ = normalize(far_ref[0:width].astype(F32))
        low = (unit * wide(scale_ref) + wide(offset_ref)).astype(BF16)
        project(low, (weight_q, weight_k, weight_v), wide(qb), wide(vb), fq.ref, fk.ref, fv.ref, (fk, fq, fv))
        x_ref = x_in()
        line = x_ref[width : width + 8, 0:width].astype(F32)
        fill_row_bias(bias, far_line, line, -2.0)
        lines.ref[0] = line
        lines.ref[1] = jnp.where(far_line < 0.0, -2.0, far_line)
        lines.go()
        grad_delta = gate_in()[:, 0:1] * wide(grad_in())
        pack.ref[1] = grad_delta.astype(BF16)
        pack.go(1)
        vec_out.ref[...] = jnp.zeros_like(vec_out.ref)
        vec_out.ref[4:5, :] = jnp.sum(wide(pack.ref.at[1]), axis=0, keepdims=True)
        store_spans(span, scalar_outs[0], scalars[0], tiles)
        q_ref, acc_ref, lse_ref = q_in(), acc_in(), lse_in()

        def work(n, j, pair):
            cols = pl.ds(pl.multiple_of(pair * PAIR, PAIR), PAIR)
            rows = pl.ds(pl.multiple_of(j * TILE, TILE), TILE)
            part, log_total = acc_ref[rows, cols], lse_ref[rows, cols]
            if n > 0:
                some = pl.ds(pl.multiple_of(span[j] * TILE, TILE), n * TILE)
                value, total, top = attend_rows(
                    q_ref[rows, cols], fk.ref[some, cols], fv.ref[some, cols], bias[rows, some]
                )
                most = jnp.maximum(top, log_total)
                far_part = jnp.exp(top - most)
                near_part = jnp.exp(log_total - most)
                total = far_part * total + near_part
                part = (part * near_part + value * far_part) / total
                log_total = most + jnp.log(total)
            attended[rows, cols] = part.astype(BF16)
            turned = log_total.T
            lse.ref[pl.ds(pair * tiles + j, 1)] = jnp.concatenate([turned[0:1], turned[HD : HD + 1]], axis=1)

        over_tiles(span, tiles, pairs, 0, work)
        pack.ref[2] = attended[...]
        pack.go(2)
        branch = nn(attended[...], ow()[...]) + wide(ob)
        branch_out.ref[...] = branch
        branch_out.go()
        unit, _ = normalize(x_ref[0:width].astype(F32) + branch)
        pack.ref[0] = (unit * wide(scale2_ref) + wide(offset2_ref)).astype(BF16)
        pack.go(0)

        second, gfl = pack.ref.at[0], pack.ref.at[1]
        for at, out in enumerate(acts):
            block = block_of(at, scalars)
            for i in range(steps):
                cols = slice(i * step, (i + 1) * step)
                start = pl.multiple_of(block * depth + i * step, step)
                pre = nn(second[...], ups[at](i)[:, cols])
                pre = pre + ub[:, pl.ds(start, step)].astype(F32)
                squared = pre * pre
                inner = pre * (0.7978845608028654 + 0.035677408136300125 * squared)
                tanh = jnp.tanh(inner)
                half = 0.5 + 0.5 * tanh
                out.ref[0, :, cols] = (pre * half).astype(BF16)
                slope = half + pre * (0.5 * (1.0 - tanh * tanh)) * (
                    0.7978845608028654 + 0.10703222440890037 * squared
                )
                grad = (nt(gfl[...], downs[at]()[cols, :]) * slope).astype(BF16)
                out.ref[1, :, cols] = grad
                vec_out.ref[pl.ds(block, 1), cols] = jnp.sum(grad.astype(F32), axis=0, keepdims=True)
            out.go()
        for start in range(0, depth, step):
            cols = slice(start, start + step)
            value = nt(acts[0].ref[1], ups[0]()[cols, :])
            for at in range(1, blocks):
                value = value + nt(acts[at].ref[1], ups[at]()[cols, :])
            back[:, cols] = value

        unit, inverse = normalize(x_ref[0:width].astype(F32) + branch_out.ref[...])
        vec_out.ref[5:6, :] = jnp.sum(back[...] * unit, axis=0, keepdims=True)
        vec_out.ref[6:7, :] = jnp.sum(back[...], axis=0, keepdims=True)
        mixed = norm_back(back[...], wide(scale2_ref), unit, inverse)
        mixed_out.ref[...] = mixed
        mixed_out.go()
        low = (gate_in()[:, 0:1] * wide(grad_in()) + mixed).astype(BF16)
        low_out.ref[...] = low
        low_out.go()
        vec_out.ref[7:8, :] = jnp.sum(low.astype(F32), axis=0, keepdims=True)
        value = nt(low, ow()[...]).astype(BF16)
        gout.ref[0:width] = value
        product = value.astype(F32) * wide(attended)
        high = product.astype(BF16)
        rest = (product - high.astype(F32)).astype(BF16)
        member = lax.broadcasted_iota(I32, (16, depth), 1) // HD
        ones = jnp.where(member == lax.broadcasted_iota(I32, (16, depth), 0), 1.0, 0.0).astype(BF16)
        delta = nt(ones, high) + nt(ones, rest)
        for head in range(H):
            for j in range(tiles):
                lot = (head // 2) * tiles + j
                at = (head % 2) * TILE
                delta_out.ref[lot : lot + 1, at : at + TILE] = delta[head : head + 1, j * TILE : (j + 1) * TILE]
        gout.ref[width:] = jnp.zeros_like(gout.ref[width:])
        for i, part in enumerate(three_parts(lse.ref[...])):
            gout.ref[width : width + lots, i * 2 * TILE : (i + 1) * 2 * TILE] = part
        for i, part in enumerate(three_parts(delta_out.ref[...])):
            gout.ref[width + extra : width + extra + lots, i * 2 * TILE : (i + 1) * 2 * TILE] = part
        gout.go()
        for start in range(0, depth, step):
            cols = slice(start, start + step)
            value = nn(acts[0].ref[0], downs[0]()[:, cols])
            for at in range(1, blocks):
                value = value + nn(acts[at].ref[0], downs[at]()[:, cols])
            feed_out.ref[:, cols] = value

    low = shape_of((width, depth), BF16)
    total = shape_of((width, depth), F32)
    stats = shape_of((lots, 2 * TILE), F32)
    return streamed(
        "far_and_feed", kernel, [spans, core],
        [query_bias, value_bias, scale, offset, out_bias, scale2, offset2, up_bias],
        [full(far)] + [columns(qkv_weight, i * depth, depth) for i in range(3)]
        + [full(a) for a in (routed, queries, acc, near_lse, gate, grad_routed, out_weight)]
        + [part(at) for at in range(blocks) for part in (up_part, down_part)],
        [low, low, low, shape_of((3, width, depth), BF16), stats, total, shape_of((2, 8, width), F32)]
        + [shape_of((2, width, depth), BF16)] * blocks
        + [total, shape_of((width + 2 * extra, depth), BF16), total, low, stats, shape_of((16, depth), F32)],
        scratch=[
            VMEM((width, width), F32), SMEM((2 * tiles,), I32), VMEM((width, depth), BF16),
            VMEM((width, depth), F32),
        ],
        scalar_outs=[shape_of((2 * tiles,), I32)],
        split=(3,),
    )


def feed_grads(got, bit, pack, far_pack, own):
    width, depth = pack.shape[1:]
    step = 256

    def kernel(scalars, small, fetches, sends, scratch, scalar_outs):
        second, own_grad, far_second, got_grad, gfl, far_gfl, own_hidden, got_hidden = fetches
        bit = scalars[0][0]

        def up(ref):
            for at in range(0, depth, step):
                cols = slice(at, at + step)
                value = tn(second()[...], own_grad()[:, cols]) + tn(far_second()[...], got_grad()[:, cols])
                ref[:, cols] = value.astype(BF16)

        def down(ref):
            for at in range(0, depth, step):
                rows = slice(at, at + step)
                value = tn(own_hidden()[:, rows], gfl()[...]) + tn(got_hidden()[:, rows], far_gfl()[...])
                ref[rows, :] = value.astype(BF16)

        up(scratch[0].at[bit])
        down(scratch[0].at[1 - bit])
        for i, out in enumerate(sends):
            source = scratch[0].at[1 - i // 2, :, pl.ds(i % 2 * half, half)]
            out.copies = [pltpu.make_async_copy(source, out.target, out.sem.at[0])]
            out.go()

    half = depth // 2
    return streamed(
        "feed_grads", kernel, [jnp.reshape(bit, (1,)).astype(I32)], [],
        [row_of(pack, 0), row_of(own, 1), row_of(far_pack, 0), row_of(got, 1),
         row_of(pack, 1), row_of(far_pack, 1), row_of(own, 0), row_of(got, 0)],
        [shape_of((depth, half), BF16)] * 4,
        scratch=[VMEM((2, depth, depth), BF16)],
    )


def own_back(part, parts, q, k, v, gout, lse, delta, fk, fv, lines, spans, far_spans):
    width, depth = q.shape
    tiles = width // TILE
    some = depth // parts
    pairs = some // PAIR
    base = part * pairs * tiles

    def kernel(scalars, small, fetches, sends, scratch, scalar_outs):
        q_in, k_in, v_in, g_in, fk_in, fv_in, lse_in, delta_in, lines_in = fetches
        dq, dk, dv = sends
        bias, far_bias, turned, far_turned, span, far_span, dq_turned = scratch
        lines_ref = lines_in()
        fill_bias(bias, lines_ref[0], lines_ref[0], -1.0)
        fill_bias(far_bias, lines_ref[1], lines_ref[0], -2.0)
        store_spans(span, scalars[0], scalars[0], tiles)
        store_spans(far_span, scalars[1], scalars[0], tiles)
        k_ref, fk_ref, q_ref, g_ref, v_ref, fv_ref = k_in(), fk_in(), q_in(), g_in(), v_in(), fv_in()
        lse_ref, delta_ref = lse_in(), delta_in()
        turned[...] = k_ref[...].T
        far_turned[...] = fk_ref[...].T
        dk.ref[...] = jnp.zeros_like(dk.ref)
        dv.ref[...] = jnp.zeros_like(dv.ref)

        def pieces(j, pair):
            cols = pl.ds(pl.multiple_of(pair * PAIR, PAIR), PAIR)
            rows = pl.ds(pl.multiple_of(j * TILE, TILE), TILE)
            query = stacked_heads(q_ref[rows, cols]) * SCALE
            grad = stacked_heads(g_ref[rows, cols])
            one = pl.ds(base + pair * tiles + j, 1)
            return cols, rows, query, grad, lse_ref[one], delta_ref[one]

        def local(n, j, pair):
            cols, rows, query, grad, top, delta = pieces(j, pair)
            near = pl.ds(pl.multiple_of(span[j] * TILE, TILE), n * TILE)
            weights = jnp.exp(nt(k_ref[near, cols], query) + twice(bias[near, rows]) - top)
            dscore = (weights * (nt(v_ref[near, cols], grad) - delta)).astype(BF16)
            dk.ref[near, cols] += nn(dscore, query)
            dv.ref[near, cols] += nn(weights.astype(BF16), grad)
            dq_turned[cols, rows] = own_blocks(nn(turned[cols, near], dscore))

        def remote(n, j, pair):
            cols, rows, query, grad, top, delta = pieces(j, pair)
            far = pl.ds(pl.multiple_of(far_span[j] * TILE, TILE), n * TILE)
            weights = jnp.exp(nt(fk_ref[far, cols], query) + twice(far_bias[far, rows]) - top)
            dscore = (weights * (nt(fv_ref[far, cols], grad) - delta)).astype(BF16)
            dq_turned[cols, rows] += own_blocks(nn(far_turned[cols, far], dscore))

        over_tiles(span, tiles, pairs, 1, local)
        over_tiles(far_span, tiles, pairs, 1, remote)
        dq.ref[...] = (dq_turned[...].T * SCALE).astype(BF16)

    total = shape_of((width, some), F32)
    return streamed(
        "own_back", kernel, [spans, far_spans], [],
        [columns(a, part * some, some) for a in (q, k, v)]
        + [(gout, lambda ref, scalars: ref.at[0:width, part * some : (part + 1) * some], (width, some))]
        + [columns(a, part * some, some) for a in (fk, fv)]
        + [full(lse), full(delta), full(lines)],
        [shape_of((width, some), BF16), total, total],
        scratch=[
            VMEM((width, width), F32), VMEM((width, width), F32),
            VMEM((some, width), BF16), VMEM((some, width), BF16),
            SMEM((2 * tiles,), I32), SMEM((2 * tiles,), I32), VMEM((some, width), F32),
        ],
    )


def other_back(fgout, core, spans, far_spans, fq, k, v, lines, grads, low, vec):
    width, depth = k.shape
    tiles = width // TILE
    parts = len(grads)
    some = depth // parts
    pairs = some // PAIR
    lots = depth // PAIR * tiles
    extra = -(-lots // 16) * 16
    half = depth // 2

    def kernel(scalars, small, fetches, sends, scratch, scalar_outs):
        g_in, fq_in, k_in, v_in, lines_in, low_in, vec_in = fetches[:7]
        pieces = fetches[7:]
        halves = sends[:4]
        dq, dk, dv, vec_out = sends[4:]
        bias, span, stat, dk_sum, dv_sum = scratch
        lines_ref = lines_in()
        fill_bias(bias, lines_ref[0], lines_ref[1], -1.0)
        store_spans(span, scalars[1], scalars[2], tiles)
        g_ref = g_in()
        for i in range(2):
            block = g_ref[width + i * extra : width + i * extra + lots]
            stat[i] = (
                block[:, 0 : 2 * TILE].astype(F32)
                + block[:, 2 * TILE : 4 * TILE].astype(F32)
                + block[:, 4 * TILE : 6 * TILE].astype(F32)
            )
        fq_ref, k_ref, v_ref = fq_in(), k_in(), v_in()
        for part in range(parts):
            place = slice(part * some, (part + 1) * some)
            dq.ref[:, place] = pieces[3 * part]()[...]
            dk_sum[:, place] = pieces[3 * part + 1]()[...]
            dv_sum[:, place] = pieces[3 * part + 2]()[...]

        def work(n, j, pair):
            cols = pl.ds(pl.multiple_of(pair * PAIR, PAIR), PAIR)
            rows = pl.ds(pl.multiple_of(j * TILE, TILE), TILE)
            one = pl.ds(pair * tiles + j, 1)
            query = stacked_heads(fq_ref[rows, cols]) * SCALE
            grad = stacked_heads(g_ref[rows, cols])
            near = pl.ds(pl.multiple_of(span[j] * TILE, TILE), n * TILE)
            scores = nt(k_ref[near, cols], query) + twice(bias[near, rows])
            weights = jnp.exp(scores - stat[0, one])
            dscore = (weights * (nt(v_ref[near, cols], grad) - stat[1, one])).astype(BF16)
            dk_sum[near, cols] += nn(dscore, query)
            dv_sum[near, cols] += nn(weights.astype(BF16), grad)

        over_tiles(span, tiles, depth // PAIR, 1, work)
        dk.ref[...] = dk_sum[...].astype(BF16)
        dv.ref[...] = dv_sum[...].astype(BF16)
        low_ref = low_in()
        cols = pl.ds(pl.multiple_of((1 - scalars[0][0]) * half, TILE), half)
        for out, ref in zip(halves, (dq.ref, dk.ref, dv.ref, low_ref)):
            out.ref[...] = ref[:, cols]
            out.go()
        vec_out.ref[...] = vec_in()[...]
        vec_out.ref[8:9, :] = jnp.sum(wide(dq.ref), axis=0, keepdims=True)
        vec_out.ref[9:10, :] = jnp.sum(wide(dv.ref), axis=0, keepdims=True)

    flat = [piece for grad in grads for piece in grad]
    low_shape = shape_of((width, depth), BF16)
    return streamed(
        "other_back", kernel, [core, spans, far_spans], [],
        [full(a) for a in (fgout, fq, k, v, lines, low, vec)] + [full(a) for a in flat],
        [shape_of((width, half), BF16)] * 4 + [low_shape] * 3 + [shape_of((16, depth), F32)],
        scratch=[
            VMEM((width, width), F32), SMEM((2 * tiles,), I32), VMEM((2, lots, 2 * TILE), F32),
            VMEM((width, depth), F32), VMEM((width, depth), F32),
        ],
    )


def last_grads(core, bit, normed, far_normed, pack, far_pack, dq, dk, dv, low, got):
    width, depth = dq.shape
    half = depth // 2

    def kernel(scalars, small, fetches, sends, scratch, scalar_outs):
        left, far_left, att, far_att, dq_in, dk_in, dv_in, low_in = fetches[:8]
        gots = fetches[8:]
        send, keep = sends
        turned = scratch[0]
        cols = pl.ds(pl.multiple_of(scalars[0][0] * half, TILE), half)
        for i, ref in enumerate((left, far_left, att, far_att)):
            turned[i // 2, :, (i % 2) * width : (i % 2 + 1) * width] = ref()[...].T
        for out, which in ((send, 1 - scalars[1][0]), (keep, scalars[1][0])):
            rows = pl.ds(pl.multiple_of(which * half, TILE), half)
            for i, part in enumerate((dq_in, dk_in, dv_in, low_in)):
                place = slice(i * half, (i + 1) * half)
                side = 0 if i < 3 else 1
                value = nn(turned[side, rows, 0:width], part()[:, cols])
                value = value + nn(turned[side, rows, width : 2 * width], gots[i]()[...])
                out.ref[:, place] = value.astype(BF16)
            out.go()

    shape = shape_of((half, 2 * depth), BF16)
    return streamed(
        "last_grads", kernel, [core, jnp.reshape(bit, (1,)).astype(I32)], [],
        [full(normed), full(far_normed), row_of(pack, 2), row_of(far_pack, 2)]
        + [full(a) for a in (dq, dk, dv, low) + tuple(got)],
        [shape, shape],
        scratch=[VMEM((2, depth, 2 * width), BF16)],
    )


def scatter(hot_ref, rows, slots_ref):
    hot = hot_ref[...]
    taken = jnp.max(hot.astype(F32), axis=-1, keepdims=True) > 0.0
    return jnp.where(taken, nn(hot, rows).astype(BF16), slots_ref[...])


def token_out(hot, tokens, routed, gate, branch, feed, down_bias, grad_routed, router, mixed, vec):
    slots, depth = tokens.shape
    width = branch.shape[0]

    def kernel(scalars, small, fetches, sends, scratch, scalar_outs):
        branch_in, feed_in, x_in, gate_in, grad_in, mixed_in, vec_in, hot_in, tok_in = fetches
        out, base, vec_out = sends
        total = branch_in()[...] + feed_in()[...] + wide(small[0])
        x = wide(x_in())
        gate = gate_in()[:, 0:1]
        grad = wide(grad_in())
        logit = jnp.sum(grad * total, axis=-1, keepdims=True) * gate * (1.0 - gate)
        base.ref[...] = grad + mixed_in()[...] + logit * wide(small[1])
        base.go()
        vec_out.ref[...] = vec_in()[...]
        vec_out.ref[12:13, :] = jnp.sum(x * logit, axis=0, keepdims=True)
        out.ref[...] = scatter(hot_in(), (x + gate * total).astype(BF16), tok_in())

    return streamed(
        "token_out", kernel, [], [down_bias, router],
        [full(branch), full(feed), head_rows(routed, width)]
        + [full(a) for a in (gate, grad_routed, mixed, vec, hot, tokens)],
        [shape_of((slots, depth), BF16), shape_of((width, depth), F32), shape_of((16, depth), F32)],
    )


def token_grad(dq, dk, dv, hot, cotangent, routed, base, scale, qkv_weight, vec):
    slots, depth = cotangent.shape
    width = base.shape[0]

    def kernel(scalars, small, fetches, sends, scratch, scalar_outs):
        dq_in, weight_q, dk_in, weight_k, dv_in, weight_v, x_in, base_in, vec_in, hot_in, cot_in = fetches
        out, vec_out = sends
        back = nt(dq_in()[...], weight_q()[...]) + nt(dk_in()[...], weight_k()[...])
        back = back + nt(dv_in()[...], weight_v()[...])
        unit, inverse = normalize(wide(x_in()))
        vec_out.ref[...] = vec_in()[...]
        vec_out.ref[10:11, :] = jnp.sum(back * unit, axis=0, keepdims=True)
        vec_out.ref[11:12, :] = jnp.sum(back, axis=0, keepdims=True)
        vec_out.go()
        rows = (base_in()[...] + norm_back(back, wide(small[0]), unit, inverse)).astype(BF16)
        out.ref[...] = scatter(hot_in(), rows, cot_in())

    return streamed(
        "token_grad", kernel, [], [scale],
        [
            full(dq), columns(qkv_weight, 0, depth), full(dk), columns(qkv_weight, depth, depth),
            full(dv), columns(qkv_weight, 2 * depth, depth), head_rows(routed, width),
            full(base), full(vec), full(hot), full(cotangent),
        ],
        [shape_of((slots, depth), BF16), shape_of((16, depth), F32)],
    )


AXES = ("rows", "seq")
SHIFT = {"c": 0, "x": 1, "z1": 2, "z2": 3}
BLOCK = 16
XY_FIRST = (("x", "y"), ("y", "x"), ("z1", "z1"), ("z2", "z2"))
YX_FIRST = (("y", "x"), ("x", "y"), ("z1", "z1"), ("z2", "z2"))


def swap(block, axes):
    route = []
    for row in range(lax.axis_size("rows")):
        axis = axes[row & 1]
        for seq in range(2):
            if axis == "y":
                other = row * 2 + (seq ^ 1)
            else:
                other = (row ^ (1 << SHIFT[axis])) * 2 + seq
            route.append((row * 2 + seq, other))
    return lax.ppermute(block, AXES, route)


def own_bit(axis):
    if axis == "y":
        return lax.axis_index("seq")
    return (lax.axis_index("rows") >> SHIFT[axis]) & 1


def stage_bit(axes, core):
    if axes[0] == axes[1]:
        return own_bit(axes[0])
    return jnp.where(core == 0, own_bit(axes[0]), own_bit(axes[1]))


def half_of(block, which):
    half = block.shape[0] // 2
    return lax.dynamic_slice_in_dim(block, which * half, half, 0)


def add_low(left, right):
    return (left.astype(F32) + right.astype(F32)).astype(BF16)


def after(value, *others):
    return lax.optimization_barrier((value, *others))[0]


def over_blocks(total):
    extra = BLOCK
    size = lax.axis_size("rows")
    while extra < size:
        route = [(i * 2 + j, (i ^ extra) * 2 + j) for i in range(size) for j in range(2)]
        got = lax.ppermute(total, AXES, route)
        total = (total.astype(F32) + got.astype(F32)).astype(total.dtype)
        extra *= 2
    return total


class Order:
    def __init__(self):
        self.tail = None

    def run(self, call, lead, *args):
        if self.tail is not None:
            leaves, tree = jax.tree.flatten(lead)
            leaves = lax.optimization_barrier(tuple(leaves) + (self.tail,))[:-1]
            lead = jax.tree.unflatten(tree, leaves)
        result = call(lead, *args)
        self.tail = jax.tree.leaves(result)[-1]
        return result


def two_parts(block):
    high = block.astype(BF16)
    return jnp.concatenate([high, (block - high.astype(F32)).astype(BF16)], axis=1)


def from_parts(block):
    half = block.shape[1] // 2
    return block[:, :half].astype(F32) + block[:, half:].astype(F32)


class Sum:
    def __init__(self, order, send, keep, stages):
        self.order, self.keep, self.stages, self.at = order, keep, stages, 1
        self.small, self.riding = None, False
        self.got = swap(send, stages[0])

    @classmethod
    def joined(cls, order, parts):
        new = cls.__new__(cls)
        new.order, new.stages, new.at = order, parts[0].stages, parts[0].at
        new.small, new.riding = None, False
        new.keep = tuple(part.keep for part in parts)
        new.got = tuple(part.got for part in parts)
        return new

    def take(self):
        if not self.riding:
            return self.got
        rows = self.got.shape[0] - self.small.shape[0]
        self.small = self.small + from_parts(self.got[rows:])
        self.riding = False
        return self.got[:rows]

    def post(self, send, axes, ride):
        if ride and self.small is not None:
            send = jnp.concatenate([send, two_parts(self.small)], axis=0)
            self.riding = True
        return swap(send, axes)

    def reduce(self):
        if self.at == len(self.stages):
            self.keep = over_blocks(self.order.run(add_low, self.take(), self.keep))
            self.got = swap(self.keep, self.stages[-1])
            return
        axes = self.stages[self.at]
        bit = stage_bit(axes, own_bit("c"))

        def add(got, keep, which):
            if isinstance(got, tuple):
                return jnp.concatenate([add(g, k, which) for g, k in zip(got, keep)], axis=1)
            return add_low(half_of(keep, which), half_of(got, which))

        arrived = self.take()
        send = self.order.run(lambda got, keep: add(got, keep, 1 - bit), arrived, self.keep)
        got = self.post(send, axes, True)
        self.keep = self.order.run(lambda got, keep: add(got, keep, bit), arrived, self.keep)
        self.got = got
        self.at += 1

    def gather(self):
        self.at -= 1
        self.keep = self.order.run(lambda got, keep: jnp.concatenate([keep, got]), self.got, self.keep)
        self.got = self.post(self.keep, self.stages[self.at - 1], self.at == 1)
        if self.at == 1:
            self.blocks = [(self.keep, 0, 0), (swap(self.keep, ("c", "c")), 1, 0)]

    def rest(self):
        self.got = self.order.run(lambda got: got, self.got)
        self.blocks += [(self.got, 0, 1), (swap(self.got, ("c", "c")), 1, 1)]
        self.take()


def shard_of(stages, core):
    index = jnp.int32(0)
    for axes in stages:
        index = index * 2 + stage_bit(axes, core)
    return index


SHARDS = 8


def place_kernel(kind, rows, count, info_ref, *rest):
    blocks = rest[:count]
    first_ref, second_ref, low, full, sems = rest[-5:]
    depth = blocks[0].shape[1]
    lots = [info_ref[3 * i + 2] for i in range(count)]
    tops = [info_ref[3 * i + 1] for i in range(count)]

    def pull(i, s):
        src = pl.ds(pl.multiple_of((s ^ info_ref[3 * i]) * rows, rows), rows)
        return pltpu.make_async_copy(blocks[i].at[src], low.at[i, pl.ds(s * rows, rows)], sems.at[0, i, s])

    def push(i, s, top):
        src = full.at[i, pl.ds(s * rows, rows)]
        lot = lots[i]
        if kind == "feed":
            copies = []
            size = depth // 2
            for t in range(2):
                at = (lot + 2 * t) * size
                if top == 0:
                    to = first_ref.at[pl.ds(s * rows, rows), pl.ds(pl.multiple_of(at, 128), size)]
                else:
                    to = second_ref.at[pl.ds(pl.multiple_of(at + s * rows, rows), rows)]
                copies.append(pltpu.make_async_copy(src.at[:, pl.ds(t * size, size)], to, sems.at[1 + t, i, s]))
            return copies
        part = depth // 4
        row = pl.ds(pl.multiple_of((tops[i] * SHARDS + s) * rows, rows), rows)
        copies = []
        for t in range(4):
            target = first_ref if t < 3 else second_ref
            at = (2 * t + lot) * part if t < 3 else lot * part
            copies.append(
                pltpu.make_async_copy(
                    src.at[:, pl.ds(t * part, part)],
                    target.at[row, pl.ds(pl.multiple_of(at, 128), part)],
                    sems.at[1 + t, i, s],
                )
            )
        return copies

    def start(i, s):
        if kind != "feed":
            for copy in push(i, s, 0):
                copy.start()
            return
        for top in range(2):

            @pl.when(tops[i] == top)
            def _(top=top):
                for copy in push(i, s, top):
                    copy.start()

    for i in range(count):
        for s in range(SHARDS):
            pull(i, s).start()
    for i in range(count):
        for s in range(SHARDS):
            pull(i, s).wait()
            dst = slice(s * rows, (s + 1) * rows)
            full[i, dst] = low[i, dst].astype(F32)
            start(i, s)
    for i in range(count):
        for s in range(SHARDS):
            for copy in push(i, s, 0):
                copy.wait()


def place(kind, rows, blocks, info, targets, shapes):
    hbm = pl.BlockSpec(memory_space=pltpu.HBM)
    targets = targets or ()
    count = len(blocks)
    return pl.pallas_call(
        functools.partial(place_kernel, kind, rows, count),
        out_shape=tuple(jax.ShapeDtypeStruct(s, F32) for s in shapes),
        in_specs=[pl.BlockSpec(memory_space=pltpu.SMEM)] + [hbm] * (count + len(targets)),
        out_specs=(hbm, hbm),
        scratch_shapes=[
            VMEM((count, rows * SHARDS, blocks[0].shape[1]), BF16),
            VMEM((count, rows * SHARDS, blocks[0].shape[1]), F32),
            pltpu.SemaphoreType.DMA((5, count, SHARDS)),
        ],
        input_output_aliases={1 + count: 0, 2 + count: 1} if targets else {},
        compiler_params=pltpu.CompilerParams(vmem_limit_bytes=62 << 20),
        cost_estimate=pl.CostEstimate(flops=int(LENGTH["place"] * RATE), bytes_accessed=0, transcendentals=0),
        name="place",
    )(info, *blocks, *targets)


def body(
    tokens,
    cotangent,
    segment_ids,
    routing,
    qkv_weight,
    query_bias,
    value_bias,
    out_weight,
    out_bias,
    first_scale,
    first_offset,
    second_scale,
    second_offset,
    up_weight,
    up_bias,
    down_weight,
    down_bias,
    router_weight,
):
    row_count, slots, depth = tokens.shape
    hidden = up_weight.shape[1]
    count = slots // 2
    width = -(-count // 128) * 128
    core = own_bit("c")
    seat = jnp.reshape(core, (1,)).astype(jnp.int32)
    pos = jnp.reshape(lax.axis_index("seq"), (1,)).astype(jnp.int32)
    tokens = tokens.reshape(slots, depth)
    cotangent = cotangent.reshape(slots, depth)
    qb, vb, ob, s1, o1, s2, o2, db, rw = (
        v.reshape(1, depth)
        for v in (query_bias, value_bias, out_bias, first_scale, first_offset, second_scale,
                  second_offset, down_bias, router_weight)
    )
    ub = up_bias.reshape(1, hidden)

    order = Order()
    routed, grad_routed, hot, spans = pick_rows(pos, routing, segment_ids, tokens, cotangent, count, width)
    far = swap(routed, ("y", "y"))
    q, k, v, normed, gate, acc, near_lse = near_attention(spans, routed, qkv_weight, qb, vb, s1, o1, rw)
    far_normed = swap(normed, ("c", "c"))
    fq, fk, fv, pack, lse, branch, lines, *rest, far_spans = order.run(
        far_and_feed, far, spans, seat, routed, qkv_weight, qb, vb, s1, o1, count, q, acc, near_lse,
        out_weight, ob, s2, o2, gate, grad_routed, up_weight, ub, down_weight
    )
    *acts, feed_sum, gout, mixed, low, delta, vec = rest
    fgout = swap(gout, ("y", "y"))
    far_pack = swap(pack, ("c", "c"))
    sends = [swap(send, ("c", "c")) for send in acts[0::2]]

    plans = (XY_FIRST, XY_FIRST, YX_FIRST)
    first_bits = [stage_bit(plan[0], core) for plan in plans]

    def feed_sums(pair):
        *out, first, second = order.run(
            feed_grads, sends[pair], first_bits[pair], pack, far_pack, acts[2 * pair + 1]
        )
        return [Sum(order, send, keep, plans[pair]) for send, keep in zip(out, (first, second))]

    def own_part(part):
        return order.run(
            lambda q: own_back(part, 2, q, k, v, gout, lse, delta, fk, fv, lines, spans, far_spans), q
        )

    out_tokens, base, vec = order.run(
        token_out, hot, tokens, routed, gate, branch, feed_sum, db, grad_routed, rw, mixed, vec
    )
    both = feed_sums(0) + feed_sums(1)
    grads = [own_part(0)]
    fgout = order.run(lambda got: got, fgout)
    both[0].got, both[1].got = order.run(lambda gots: gots, (both[0].got, both[1].got))
    grads.append(own_part(1))
    both = Sum.joined(order, both)
    both.reduce()
    *last_sends, dq, dk, dv, vec = order.run(
        other_back, fgout, seat, spans, far_spans, fq, k, v, lines, grads, low, vec
    )
    gots = [swap(send, ("c", "c")) for send in last_sends]
    both.reduce()
    send, keep = order.run(
        lambda got, *rest: last_grads(
            seat, first_bits[2], normed, far_normed, pack, far_pack, dq, dk, dv, low, (got,) + rest
        ), *gots
    )
    three = Sum(order, send, keep, plans[2])
    grad_tokens, vec = order.run(token_grad, dq, dk, dv, hot, cotangent, routed, base, s1, qkv_weight, vec)
    three.small = vec

    kinds = {
        "feed": ((depth, hidden), (hidden, depth)),
        "last": ((depth, 3 * depth), (depth, depth)),
    }
    targets = {"feed": None, "last": None}
    rows = {"feed": depth // 8, "last": depth // 16}

    def put(kind, some):
        blocks, info = [], []
        for block, other, half in some:
            owner = core if other == 0 else 1 - core
            own = shard_of(plans[0] if kind == "feed" else plans[2], owner)
            blocks.append(block)
            info += [own % 8, own // 8 ^ half, owner]
        info = jnp.stack(info).astype(jnp.int32)
        targets[kind] = order.run(
            lambda block, *rest: place(kind, rows[kind], rest + (block,), info, targets[kind], kinds[kind]),
            blocks[-1], *blocks[:-1]
        )

    both.reduce()
    both.reduce()
    three.reduce()
    both.gather()
    three.reduce()
    both.gather()
    three.reduce()
    three.reduce()
    both.gather()
    three.gather()
    put("feed", both.blocks[:2])
    three.gather()
    both.rest()
    three.gather()
    put("last", three.blocks)
    put("feed", both.blocks[2:])
    three.rest()
    vec = three.small + swap(three.small, ("c", "c"))
    put("last", three.blocks[2:3])
    put("last", three.blocks[3:])
    vec = over_blocks(vec)
    grad_up, grad_down = targets["feed"]
    grad_qkv, grad_out = targets["last"]
    return (
        out_tokens.reshape(row_count, slots, depth),
        grad_tokens.reshape(row_count, slots, depth),
        grad_qkv,
        vec[8],
        vec[9],
        grad_out,
        vec[7],
        vec[10],
        vec[11],
        vec[5],
        vec[6],
        grad_up,
        vec[0:4].reshape(hidden),
        grad_down,
        vec[4],
        vec[12],
    )


def solution(mesh):
    split = P("rows", "seq", None)
    return jax.shard_map(
        body,
        mesh=mesh,
        in_specs=(split, split, P("rows", None), P("rows", None)) + (P(),) * 14,
        out_specs=(split, split) + (P(),) * 14,
        check_vma=False,
    )
```
